32 devices in a mesh: rep: 4 (over y, core), shard: 4 (over z), ctx: 2 (over x).
Axes of the slice: x: 2, y: 2, z: 4, core: 2. Of those that a mesh axis runs over, the one named last changes fastest.
Arguments:
- tokens: bfloat16 [16, 256, 1024], P(('rep', 'shard'), 'ctx'), may hold values from -6 to 6
- out_grad: bfloat16 [16, 256, 1024], P(('rep', 'shard'), 'ctx'), may hold values from -6 to 6
- positions: int32 [16, 256], P(('rep', 'shard'), 'ctx'), may hold values from 0 to 255, as said below
- stretch_order: int32 [4], replicated, may hold values from 0 to 3, as said below
- attn_gain: bfloat16 [1024], P(('shard', 'ctx')), may hold values from 0.099609375 to 1.8984375
- query_gain: bfloat16 [128], replicated, may hold values from 0.5 to 6
- key_norm_gain: bfloat16 [128], replicated, may hold values from 0.5 to 6
- query_weight: bfloat16 [1024, 2048], P(('shard', 'ctx')), may hold values from -0.1875 to 0.1875
- key_projection_matrix: bfloat16 [1024, 1024], P(('shard', 'ctx')), may hold values from -0.1875 to 0.1875
- value_projection_matrix: bfloat16 [1024, 1024], P(('shard', 'ctx')), may hold values from -0.1875 to 0.1875
- output_weight: bfloat16 [1024, 2048], P(('shard', 'ctx')), may hold values from -0.375 to 0.375
- ffn_gain: bfloat16 [1024], P(('shard', 'ctx')), may hold values from 0.099609375 to 1.8984375
- gate_weight: bfloat16 [1024, 3072], P(('shard', 'ctx')), may hold values from -0.1875 to 0.1875
- up_weight: bfloat16 [1024, 3072], P(('shard', 'ctx')), may hold values from -0.1875 to 0.1875
- down_weight: bfloat16 [1024, 3072], P(('shard', 'ctx')), may hold values from -0.109375 to 0.109375
Outputs:
- block_out: bfloat16 [16, 256, 1024], P(('rep', 'shard'), 'ctx')
- tokens_grad: float32 [16, 256, 1024], P(('rep', 'shard'), 'ctx')
- query_weight_grad: float32 [1024, 2048], P(('shard', 'ctx'))
- key_weight_grad: float32 [1024, 1024], P(('shard', 'ctx'))
- value_weight_grad: float32 [1024, 1024], P(('shard', 'ctx'))
- output_weight_grad: float32 [1024, 2048], P(('shard', 'ctx'))
- gate_weight_grad: float32 [1024, 3072], P(('shard', 'ctx'))
- up_weight_grad: float32 [1024, 3072], P(('shard', 'ctx'))
- down_weight_grad: float32 [1024, 3072], P(('shard', 'ctx'))
- attn_gain_grad: float32 [1024], P(('shard', 'ctx'))
- ffn_gain_grad: float32 [1024], P(('shard', 'ctx'))
- query_gain_grad: float32 [128], replicated
- key_gain_grad: float32 [128], replicated
The draws below stay inside these ranges and needn't reach their ends.
Inputs may be any that keep to these rules, and one draw needn't show every extreme that they name: A permutation: stored block j of every sequence holds sequence block stretch_order[j], each block 64 tokens. In sequence order (see stretch_order) the positions of a sequence start at 0, rise by one from token to token and restart at 0 where a packed document starts; sequence 0 holds one document.
All inputs are finite; a program needn't handle non-finite values.
Results may differ from the reference program's by a relative error of at most 0.019.
The reference program's roundings to bfloat16 on the way count: a program that leaves them out, or rounds other values in their place, can miss the bound.
Values may be sent and summed in bfloat16 or wider, within the bound.
No kernel may reach another device: no remote copies, remote signals or barrier semaphores. Data moves between devices by JAX's collectives and lax.ppermute only.
A program may use at most 256 MiB of HBM per device.

```python
import math
import jax
import jax.numpy as jnp
from jax import lax

MODEL_FEATURES = 1024
QUERY_HEADS = 16
KEY_VALUE_HEADS = 8
HEAD_SIZE = 128
FEEDFORWARD_UNITS = 3072
STRETCH = 64
BLOCKS = 4
SEQUENCE_LENGTH = 256
SEQS = 16


def stored_order(key):
    return jax.random.permutation(jax.random.fold_in(key, 7), BLOCKS).astype(jnp.int32)


def draw_stretch_order(key, part):
    return stored_order(key)


def draw_positions(key, part):
    order = stored_order(key)
    places = jnp.arange(SEQUENCE_LENGTH, dtype=jnp.int32)
    starts = jax.random.randint(jax.random.fold_in(key, 11), (SEQS, SEQUENCE_LENGTH), 0, 64) == 0
    starts = starts.at[:, 0].set(True)
    starts = starts.at[0, :].set(False)
    starts = starts.at[0, 0].set(True)
    marks = jnp.where(starts, places[None, :], 0)
    latest = lax.cummax(marks, axis=1)
    natural = places[None, :] - latest
    stored = natural.reshape(SEQS, BLOCKS, STRETCH)[:, order, :]
    return stored.reshape(SEQS, SEQUENCE_LENGTH).astype(jnp.int32)


def draw_query_gain(key, part):
    values = jnp.exp(jax.random.uniform(jax.random.fold_in(key, 3), (HEAD_SIZE,), jnp.float32, math.log(0.5), math.log(2.0)))
    return values.astype(jnp.bfloat16)


def draw_key_norm_gain(key, part):
    values = jnp.exp(jax.random.uniform(jax.random.fold_in(key, 5), (HEAD_SIZE,), jnp.float32, math.log(0.5), math.log(2.0)))
    return values.astype(jnp.bfloat16)


def shard_levels(key, extent, shards, smallest, largest):
    gain = 1.0
    for dim, shards_of in shards:
        heights = jax.random.uniform(jax.random.fold_in(jax.random.fold_in(key, 6), dim), (shards_of,), jnp.float32, smallest / len(shards), largest / len(shards))
        gain = gain * jnp.repeat(jnp.exp(heights), extent[dim] // shards_of).reshape((-1,) + (1,) * (len(extent) - 1 - dim))
    return gain


def scatter_about(rng, shape, spread, bound, cuts=(), held_as=jnp.bfloat16):
    values = jax.random.normal(rng, shape, jnp.float32) * spread
    if len(cuts) > 0:
        values = shard_levels(rng, shape, cuts, -0.22, 0.18) * values
    return jnp.clip(values, min=-bound, max=bound).astype(held_as)


def setup_inputs(seed: int = 0) -> dict:
    keys = jax.random.split(jax.random.key(seed), 16)
    return {
        "tokens": scatter_about(keys[0], (SEQS, SEQUENCE_LENGTH, MODEL_FEATURES), 1.0, 6.0, ((0, 16), (1, 2))),
        "out_grad": scatter_about(keys[1], (SEQS, SEQUENCE_LENGTH, MODEL_FEATURES), 1.0, 6.0, ((0, 16), (1, 2))),
        "positions": draw_positions(jax.random.fold_in(keys[15], 71), 0),
        "stretch_order": draw_stretch_order(jax.random.fold_in(keys[15], 71), 0),
        "attn_gain": jnp.clip(1.0 + 0.18 * jax.random.normal(keys[4], (MODEL_FEATURES,), jnp.float32), 0.099609375, 1.8984375).astype(jnp.bfloat16),
        "query_gain": draw_query_gain(jax.random.fold_in(keys[15], 71), 0),
        "key_norm_gain": draw_key_norm_gain(jax.random.fold_in(keys[15], 71), 0),
        "query_weight": scatter_about(keys[7], (MODEL_FEATURES, QUERY_HEADS * HEAD_SIZE), MODEL_FEATURES ** -0.5, 0.1875, ((0, 8),)),
        "key_projection_matrix": scatter_about(keys[8], (MODEL_FEATURES, KEY_VALUE_HEADS * HEAD_SIZE), MODEL_FEATURES ** -0.5, 0.1875, ((0, 8),)),
        "value_projection_matrix": scatter_about(keys[9], (MODEL_FEATURES, KEY_VALUE_HEADS * HEAD_SIZE), MODEL_FEATURES ** -0.5, 0.1875, ((0, 8),)),
        "output_weight": scatter_about(keys[10], (MODEL_FEATURES, QUERY_HEADS * HEAD_SIZE), (QUERY_HEADS * HEAD_SIZE // 8) ** -0.5, 0.375, ((0, 8),)),
        "ffn_gain": jnp.clip(1.0 + 0.18 * jax.random.normal(keys[11], (MODEL_FEATURES,), jnp.float32), 0.099609375, 1.8984375).astype(jnp.bfloat16),
        "gate_weight": scatter_about(keys[12], (MODEL_FEATURES, FEEDFORWARD_UNITS), MODEL_FEATURES ** -0.5, 0.1875, ((0, 8),)),
        "up_weight": scatter_about(keys[13], (MODEL_FEATURES, FEEDFORWARD_UNITS), MODEL_FEATURES ** -0.5, 0.1875, ((0, 8),)),
        "down_weight": scatter_about(keys[14], (MODEL_FEATURES, FEEDFORWARD_UNITS), FEEDFORWARD_UNITS ** -0.5, 0.109375, ((0, 8),)),
    }


EPSILON = 1e-06
ROPE_THETA = 1000000.0
NEGATIVE = -1e+30

def plain_product(left_side, right_side):
    return jnp.dot(left_side, right_side, preferred_element_type=jnp.float32)

def dot_right(left_side, right_side):
    return lax.dot_general(left_side, right_side, (((1,), (1,)), ((), ())), preferred_element_type=jnp.float32)

def dot_left(left_side, right_side):
    return lax.dot_general(left_side, right_side, (((0,), (0,)), ((), ())), preferred_element_type=jnp.float32)

def rope_tables(positions, head_width):
    half_width = head_width // 2
    freq_steps = jnp.arange(half_width, dtype=jnp.float32)
    inverse = jnp.exp(freq_steps * (-2.0 * math.log(ROPE_THETA) / head_width))
    angles = positions.astype(jnp.float32)[..., None] * inverse
    return (jnp.cos(angles)[..., None, :], jnp.sin(angles)[..., None, :])

def apply_rotation(values, cosine_values, sine_values):
    half_width = values.shape[-1] // 2
    front_half = values[..., :half_width]
    back_half = values[..., half_width:]
    return jnp.concatenate([front_half * cosine_values - back_half * sine_values, back_half * cosine_values + front_half * sine_values], axis=-1)

def reverse_rotation(gradient, cosine_values, sine_values):
    half_width = gradient.shape[-1] // 2
    front_half = gradient[..., :half_width]
    back_half = gradient[..., half_width:]
    return jnp.concatenate([front_half * cosine_values + back_half * sine_values, back_half * cosine_values - front_half * sine_values], axis=-1)

def per_head_norm(values, gain_vector):
    inverse_rms = lax.rsqrt(lax.optimization_barrier(jnp.mean(values * values, axis=-1, keepdims=True)) + EPSILON)
    unit_vector = values * inverse_rms
    return (unit_vector * gain_vector.astype(jnp.float32), unit_vector, inverse_rms)

def per_head_norm_backward(gradient, unit_vector, inverse_rms, gain_vector):
    gain_grad = lax.optimization_barrier(jnp.sum(gradient * unit_vector, axis=tuple(range(gradient.ndim - 1))))
    scaled = gradient * gain_vector.astype(jnp.float32)
    return (gain_grad, inverse_rms * (scaled - unit_vector * lax.optimization_barrier(jnp.mean(scaled * unit_vector, axis=-1, keepdims=True))))

def attention_scores(query_heads, key_heads, visible):
    scores = jnp.einsum('sqgrd,skgd->sgrqk', query_heads.astype(jnp.float32), key_heads.astype(jnp.float32)) * (1.0 / math.sqrt(HEAD_SIZE))
    return jnp.where(visible, scores, NEGATIVE)

def attend(query_rot, key_rotated, value_row_matrix, visible, group_length):
    sequence_batch, query_count = (query_rot.shape[0], query_rot.shape[1])
    key_count = key_rotated.shape[1]
    kv_heads = key_rotated.shape[2] // HEAD_SIZE
    query_heads = query_rot.reshape(sequence_batch, query_count, kv_heads, group_length, HEAD_SIZE)
    key_heads = key_rotated.reshape(sequence_batch, key_count, kv_heads, HEAD_SIZE)
    value_heads = value_row_matrix.reshape(sequence_batch, key_count, kv_heads, HEAD_SIZE)
    scores = attention_scores(query_heads, key_heads, visible)
    row_max = lax.optimization_barrier(jnp.max(scores, axis=-1, keepdims=True))
    log_total = row_max + jnp.log(lax.optimization_barrier(jnp.sum(jnp.exp(scores - row_max), axis=-1, keepdims=True)))
    attention_probs = jnp.exp(scores - log_total).astype(jnp.bfloat16)
    attended = jnp.einsum('sgrqk,skgd->sqgrd', attention_probs.astype(jnp.float32), value_heads.astype(jnp.float32))
    return (attended.astype(jnp.bfloat16).reshape(sequence_batch, query_count, kv_heads * group_length * HEAD_SIZE), log_total)

def attend_back(query_rot, key_rotated, value_row_matrix, attended, attended_grad, log_total, visible, group_length):
    sequence_batch, query_count = (query_rot.shape[0], query_rot.shape[1])
    key_count = key_rotated.shape[1]
    kv_heads = key_rotated.shape[2] // HEAD_SIZE
    query_heads = query_rot.reshape(sequence_batch, query_count, kv_heads, group_length, HEAD_SIZE).astype(jnp.float32)
    key_heads = key_rotated.reshape(sequence_batch, key_count, kv_heads, HEAD_SIZE).astype(jnp.float32)
    value_heads = value_row_matrix.reshape(sequence_batch, key_count, kv_heads, HEAD_SIZE).astype(jnp.float32)
    scores = attention_scores(query_heads, key_heads, visible)
    prob_float = jnp.exp(scores - log_total)
    attention_probs = prob_float.astype(jnp.bfloat16).astype(jnp.float32)
    grad_heads = attended_grad.reshape(sequence_batch, query_count, kv_heads, group_length, HEAD_SIZE).astype(jnp.float32)
    output_heads = attended.reshape(sequence_batch, query_count, kv_heads, group_length, HEAD_SIZE).astype(jnp.float32)
    row_delta = jnp.einsum('sqgrd,sqgrd->sgrq', grad_heads, output_heads)
    value_gradient = jnp.einsum('sgrqk,sqgrd->skgd', attention_probs, grad_heads)
    prob_grad = jnp.einsum('sqgrd,skgd->sgrqk', grad_heads, value_heads)
    score_grad = (prob_float * (prob_grad - row_delta[..., None])).astype(jnp.bfloat16).astype(jnp.float32)
    scale_factor = 1.0 / math.sqrt(HEAD_SIZE)
    query_grad = jnp.einsum('sgrqk,skgd->sqgrd', score_grad, key_heads) * scale_factor
    key_gradient = jnp.einsum('sgrqk,sqgrd->skgd', score_grad, query_heads) * scale_factor
    return (query_grad.reshape(sequence_batch, query_count, kv_heads * group_length * HEAD_SIZE), key_gradient.reshape(sequence_batch, key_count, kv_heads * HEAD_SIZE), value_gradient.reshape(sequence_batch, key_count, kv_heads * HEAD_SIZE))

def reference(tokens, out_grad, positions, stretch_order, attn_gain, query_gain, key_norm_gain, query_weight, key_projection_matrix, value_projection_matrix, output_weight, ffn_gain, gate_weight, up_weight, down_weight):
    group_length = math.gcd(SEQS, 16)
    block_count = SEQS // group_length
    places = jnp.arange(SEQUENCE_LENGTH, dtype=jnp.int32)
    block_match = (places // STRETCH)[:, None] == jnp.arange(BLOCKS, dtype=jnp.int32)[None, :]
    seq_index = lax.optimization_barrier(jnp.sum(jnp.where(block_match, stretch_order[None, :], 0), axis=1)) * STRETCH + places % STRETCH
    visible = seq_index[None, :] <= seq_index[:, None]
    grouped_heads = QUERY_HEADS // KEY_VALUE_HEADS

    def one_block(running, inputs):
        block_tokens, block_grad, block_positions = inputs
        total_rows = group_length * SEQUENCE_LENGTH
        flat_tokens = block_tokens.reshape(total_rows, MODEL_FEATURES).astype(jnp.float32)
        inv_first = lax.rsqrt(lax.optimization_barrier(jnp.mean(flat_tokens * flat_tokens, axis=1, keepdims=True)) + EPSILON)
        unit_first = flat_tokens * inv_first
        first_normalized = (unit_first * attn_gain.astype(jnp.float32)).astype(jnp.bfloat16)
        query = plain_product(first_normalized, query_weight)
        key = plain_product(first_normalized, key_projection_matrix)
        value_row_matrix = plain_product(first_normalized, value_projection_matrix).astype(jnp.bfloat16).reshape(group_length, SEQUENCE_LENGTH, KEY_VALUE_HEADS * HEAD_SIZE)
        cosine_values, sine_values = rope_tables(block_positions, HEAD_SIZE)
        query_scaled, query_unit, query_inv = per_head_norm(query.reshape(group_length, SEQUENCE_LENGTH, QUERY_HEADS, HEAD_SIZE), query_gain)
        key_gain_scaled, key_normalized, key_inverse_norm = per_head_norm(key.reshape(group_length, SEQUENCE_LENGTH, KEY_VALUE_HEADS, HEAD_SIZE), key_norm_gain)
        query_rot = apply_rotation(query_scaled, cosine_values, sine_values).astype(jnp.bfloat16).reshape(group_length, SEQUENCE_LENGTH, QUERY_HEADS * HEAD_SIZE)
        key_rotated = apply_rotation(key_gain_scaled, cosine_values, sine_values).astype(jnp.bfloat16).reshape(group_length, SEQUENCE_LENGTH, KEY_VALUE_HEADS * HEAD_SIZE)
        attended, log_total = attend(query_rot, key_rotated, value_row_matrix, visible, grouped_heads)
        attended_flat = attended.reshape(total_rows, QUERY_HEADS * HEAD_SIZE)
        middle = flat_tokens + dot_right(attended_flat, output_weight)
        inv_second = lax.rsqrt(lax.optimization_barrier(jnp.mean(middle * middle, axis=1, keepdims=True)) + EPSILON)
        unit_second = middle * inv_second
        normed_second = (unit_second * ffn_gain.astype(jnp.float32)).astype(jnp.bfloat16)
        gate_value = plain_product(normed_second, gate_weight)
        up_value = plain_product(normed_second, up_weight)
        sigmoid_gate = jax.nn.sigmoid(gate_value)
        activated = gate_value * sigmoid_gate
        hidden = (activated * up_value).astype(jnp.bfloat16)
        block_out = (middle + dot_right(hidden, down_weight)).astype(jnp.bfloat16)
        grad_rows = block_grad.reshape(total_rows, MODEL_FEATURES)
        down_term = dot_left(grad_rows, hidden)
        hidden_grad = plain_product(grad_rows, down_weight)
        gate_grad = (hidden_grad * up_value * sigmoid_gate * (1.0 + gate_value * (1.0 - sigmoid_gate))).astype(jnp.bfloat16)
        up_grad = (hidden_grad * activated).astype(jnp.bfloat16)
        gate_term = dot_left(normed_second, gate_grad)
        up_term = dot_left(normed_second, up_grad)
        normed_grad_second = dot_right(gate_grad, gate_weight) + dot_right(up_grad, up_weight)
        ffn_gain_term = lax.optimization_barrier(jnp.sum(normed_grad_second * unit_second, axis=0))
        unit_grad_second = normed_grad_second * ffn_gain.astype(jnp.float32)
        middle_grad = grad_rows.astype(jnp.float32) + inv_second * (unit_grad_second - unit_second * lax.optimization_barrier(jnp.mean(unit_grad_second * unit_second, axis=1, keepdims=True)))
        middle_grad_b = middle_grad.astype(jnp.bfloat16)
        output_term = dot_left(middle_grad_b, attended_flat)
        attended_grad = plain_product(middle_grad_b, output_weight).astype(jnp.bfloat16)
        query_grad, key_gradient, value_gradient = attend_back(query_rot, key_rotated, value_row_matrix, attended, attended_grad.reshape(group_length, SEQUENCE_LENGTH, QUERY_HEADS * HEAD_SIZE), log_total, visible, grouped_heads)
        query_gain_term, query_pre = per_head_norm_backward(reverse_rotation(query_grad.reshape(group_length, SEQUENCE_LENGTH, QUERY_HEADS, HEAD_SIZE), cosine_values, sine_values), query_unit, query_inv, query_gain)
        key_gain_contribution, key_projected = per_head_norm_backward(reverse_rotation(key_gradient.reshape(group_length, SEQUENCE_LENGTH, KEY_VALUE_HEADS, HEAD_SIZE), cosine_values, sine_values), key_normalized, key_inverse_norm, key_norm_gain)
        query_grad_b = query_pre.reshape(total_rows, QUERY_HEADS * HEAD_SIZE).astype(jnp.bfloat16)
        key_gradient_second = key_projected.reshape(total_rows, KEY_VALUE_HEADS * HEAD_SIZE).astype(jnp.bfloat16)
        value_gradient_second = value_gradient.reshape(total_rows, KEY_VALUE_HEADS * HEAD_SIZE).astype(jnp.bfloat16)
        query_term = dot_left(first_normalized, query_grad_b)
        key_term = dot_left(first_normalized, key_gradient_second)
        value_term = dot_left(first_normalized, value_gradient_second)
        normed_grad_first = dot_right(query_grad_b, query_weight) + dot_right(key_gradient_second, key_projection_matrix) + dot_right(value_gradient_second, value_projection_matrix)
        attn_gain_term = lax.optimization_barrier(jnp.sum(normed_grad_first * unit_first, axis=0))
        unit_grad_first = normed_grad_first * attn_gain.astype(jnp.float32)
        tokens_grad = middle_grad + inv_first * (unit_grad_first - unit_first * lax.optimization_barrier(jnp.mean(unit_grad_first * unit_first, axis=1, keepdims=True)))
        terms = (query_term, key_term, value_term, output_term, gate_term, up_term, down_term, attn_gain_term, ffn_gain_term, query_gain_term, key_gain_contribution)
        return (jax.tree.map(jnp.add, running, terms), (block_out.reshape(group_length, SEQUENCE_LENGTH, MODEL_FEATURES), tokens_grad.reshape(group_length, SEQUENCE_LENGTH, MODEL_FEATURES)))
    starting_values = (jnp.zeros((MODEL_FEATURES, QUERY_HEADS * HEAD_SIZE), jnp.float32), jnp.zeros((MODEL_FEATURES, KEY_VALUE_HEADS * HEAD_SIZE), jnp.float32), jnp.zeros((MODEL_FEATURES, KEY_VALUE_HEADS * HEAD_SIZE), jnp.float32), jnp.zeros((MODEL_FEATURES, QUERY_HEADS * HEAD_SIZE), jnp.float32), jnp.zeros((MODEL_FEATURES, FEEDFORWARD_UNITS), jnp.float32), jnp.zeros((MODEL_FEATURES, FEEDFORWARD_UNITS), jnp.float32), jnp.zeros((MODEL_FEATURES, FEEDFORWARD_UNITS), jnp.float32), jnp.zeros((MODEL_FEATURES,), jnp.float32), jnp.zeros((MODEL_FEATURES,), jnp.float32), jnp.zeros((HEAD_SIZE,), jnp.float32), jnp.zeros((HEAD_SIZE,), jnp.float32))
    inputs = (tokens.reshape(block_count, group_length, SEQUENCE_LENGTH, MODEL_FEATURES), out_grad.reshape(block_count, group_length, SEQUENCE_LENGTH, MODEL_FEATURES), positions.reshape(block_count, group_length, SEQUENCE_LENGTH))
    totals, (outputs, input_grads) = lax.scan(one_block, starting_values, inputs)
    return (outputs.reshape(SEQS, SEQUENCE_LENGTH, MODEL_FEATURES), input_grads.reshape(SEQS, SEQUENCE_LENGTH, MODEL_FEATURES), totals[0], totals[1], totals[2], totals[3], totals[4], totals[5], totals[6], totals[7], totals[8], totals[9], totals[10])
```

```python
import math

import jax
import jax.numpy as jnp
from jax import lax
from jax.sharding import PartitionSpec as P

QUERY_HEADS = 16
KEY_VALUE_HEADS = 8
HEAD_SIZE = 128


EPSILON = 1e-06
ROPE_THETA = 1000000.0
NEGATIVE = -1e30


def plain_product(left_side, right_side):
    return jnp.dot(left_side, right_side, preferred_element_type=jnp.float32)


def dot_right(left_side, right_side):
    return lax.dot_general(
        left_side, right_side, (((1,), (1,)), ((), ())), preferred_element_type=jnp.float32
    )


def dot_left(left_side, right_side):
    return lax.dot_general(
        left_side, right_side, (((0,), (0,)), ((), ())), preferred_element_type=jnp.float32
    )


def rope_tables(positions, head_width):
    half_width = head_width // 2
    freq_steps = jnp.arange(half_width, dtype=jnp.float32)
    inverse = jnp.exp(freq_steps * (-2.0 * math.log(ROPE_THETA) / head_width))
    angles = positions.astype(jnp.float32)[..., None] * inverse
    return (jnp.cos(angles)[..., None, :], jnp.sin(angles)[..., None, :])


def apply_rotation(values, cosine_values, sine_values):
    half_width = values.shape[-1] // 2
    front_half = values[..., :half_width]
    back_half = values[..., half_width:]
    return jnp.concatenate(
        [
            front_half * cosine_values - back_half * sine_values,
            back_half * cosine_values + front_half * sine_values,
        ],
        axis=-1,
    )


def reverse_rotation(gradient, cosine_values, sine_values):
    half_width = gradient.shape[-1] // 2
    front_half = gradient[..., :half_width]
    back_half = gradient[..., half_width:]
    return jnp.concatenate(
        [
            front_half * cosine_values + back_half * sine_values,
            back_half * cosine_values - front_half * sine_values,
        ],
        axis=-1,
    )


def per_head_norm(values, gain_vector):
    inverse_rms = lax.rsqrt(jnp.mean(values * values, axis=-1, keepdims=True) + EPSILON)
    unit_vector = values * inverse_rms
    return (unit_vector * gain_vector.astype(jnp.float32), unit_vector, inverse_rms)


def per_head_norm_backward(gradient, unit_vector, inverse_rms, gain_vector):
    gain_grad = jnp.sum(gradient * unit_vector, axis=tuple(range(gradient.ndim - 1)))
    scaled = gradient * gain_vector.astype(jnp.float32)
    return (
        gain_grad,
        inverse_rms
        * (scaled - unit_vector * jnp.mean(scaled * unit_vector, axis=-1, keepdims=True)),
    )


def peer_of(index, step, size):
    if size & (size - 1) == 0:
        return index ^ step
    return (index + step) % size


def gather_blocks(value, axis_name):
    size = lax.axis_size(axis_name)
    blocks = [value]
    for step in range(1, size):
        pairs = [(peer_of(index, step, size), index) for index in range(size)]
        blocks.append(lax.ppermute(value, axis_name, pairs))
    return blocks


def scatter_sum(parts, axis_name):
    size = lax.axis_size(axis_name)
    total = parts[0]
    for step in range(1, size):
        pairs = [(index, peer_of(index, step, size)) for index in range(size)]
        moved = lax.ppermute(parts[step].astype(jnp.bfloat16), axis_name, pairs)
        total = total + moved.astype(jnp.float32)
    return total


def block_source(axis_name, step):
    return peer_of(lax.axis_index(axis_name), step, lax.axis_size(axis_name))


def split_rows(value, count):
    rows = value.shape[0] // count
    return [value[place * rows : (place + 1) * rows] for place in range(count)]


def column_slice(matrix, place, count):
    width = matrix.shape[1] // count
    return lax.dynamic_slice_in_dim(matrix, place * width, width, axis=1)


def masked_scores(query_heads, key_heads, visible):
    scores = jnp.einsum(
        "sqgrd,skgd->sgrqk", query_heads, key_heads, preferred_element_type=jnp.float32
    ) * (1.0 / math.sqrt(HEAD_SIZE))
    return jnp.where(visible, scores, NEGATIVE)


def attend(query_heads, key_heads, value_heads, visible):
    scores = masked_scores(query_heads, key_heads, visible)
    row_max = jnp.max(scores, axis=-1, keepdims=True)
    log_total = row_max + jnp.log(jnp.sum(jnp.exp(scores - row_max), axis=-1, keepdims=True))
    attention_probs = jnp.exp(scores - log_total).astype(jnp.bfloat16)
    attended = jnp.einsum(
        "sgrqk,skgd->sqgrd", attention_probs, value_heads, preferred_element_type=jnp.float32
    ).astype(jnp.bfloat16)
    return (attended, log_total)


def attend_back(query_heads, key_heads, value_heads, attended, attended_grad, log_total, visible):
    scores = masked_scores(query_heads, key_heads, visible)
    prob_float = jnp.exp(scores - log_total)
    attention_probs = prob_float.astype(jnp.bfloat16)
    row_delta = jnp.einsum(
        "sqgrd,sqgrd->sgrq", attended_grad, attended, preferred_element_type=jnp.float32
    )
    value_gradient = jnp.einsum(
        "sgrqk,sqgrd->skgd", attention_probs, attended_grad, preferred_element_type=jnp.float32
    )
    prob_grad = jnp.einsum(
        "sqgrd,skgd->sgrqk", attended_grad, value_heads, preferred_element_type=jnp.float32
    )
    score_grad = (prob_float * (prob_grad - row_delta[..., None])).astype(jnp.bfloat16)
    scale_factor = 1.0 / math.sqrt(HEAD_SIZE)
    query_grad = (
        jnp.einsum("sgrqk,skgd->sqgrd", score_grad, key_heads, preferred_element_type=jnp.float32)
        * scale_factor
    )
    key_gradient = (
        jnp.einsum("sgrqk,sqgrd->skgd", score_grad, query_heads, preferred_element_type=jnp.float32)
        * scale_factor
    )
    return (query_grad, key_gradient, value_gradient)


def per_device(
    tokens,
    out_grad,
    positions,
    stretch_order,
    attn_gain,
    query_gain,
    key_norm_gain,
    query_weight,
    key_projection_matrix,
    value_projection_matrix,
    output_weight,
    ffn_gain,
    gate_weight,
    up_weight,
    down_weight,
):
    owners = ("shard", "ctx")
    sequence_batch, count_of_rows, model_width = tokens.shape
    local_rows = sequence_batch * count_of_rows
    members = lax.axis_size("rep")
    own_member = lax.axis_index("rep")
    ctx_size = lax.axis_size("ctx")
    sequences = members * sequence_batch
    total_rows = members * local_rows
    query_heads_here = QUERY_HEADS // members
    kv_heads_here = KEY_VALUE_HEADS // members
    grouped_heads = QUERY_HEADS // KEY_VALUE_HEADS
    query_width = query_heads_here * HEAD_SIZE
    kv_width = kv_heads_here * HEAD_SIZE
    hidden_width = gate_weight.shape[1] // members
    own_rows = model_width // lax.axis_size(owners)
    own_start = lax.axis_index(owners) * own_rows

    def part(matrix):
        return column_slice(matrix, own_member, members)

    full_qkv = lax.all_gather(
        jnp.concatenate(
            [part(query_weight), part(key_projection_matrix), part(value_projection_matrix)],
            axis=1,
        ),
        owners,
        axis=0,
        tiled=True,
    )
    full_output = lax.all_gather(part(output_weight), owners, axis=0, tiled=True)
    full_gate_up = lax.all_gather(
        jnp.concatenate([part(gate_weight), part(up_weight)], axis=1), owners, axis=0, tiled=True
    )
    full_down = lax.all_gather(part(down_weight), owners, axis=0, tiled=True)
    gains = lax.all_gather(jnp.stack([attn_gain, ffn_gain]), owners, axis=1, tiled=True).astype(
        jnp.float32
    )
    full_gain = gains[0][None, :]
    full_ffn_gain = gains[1][None, :]

    own_tokens = tokens.reshape(local_rows, model_width)
    own_grads = out_grad.reshape(local_rows, model_width)
    all_tokens = jnp.concatenate(gather_blocks(own_tokens, "rep"), axis=0)
    all_grads = jnp.concatenate(gather_blocks(own_grads, "rep"), axis=0)
    all_positions = jnp.concatenate(gather_blocks(positions, "rep"), axis=0)
    cosine_values, sine_values = rope_tables(all_positions, HEAD_SIZE)

    block_count = stretch_order.shape[0]
    stretches_here = block_count // ctx_size
    block_rows = count_of_rows // stretches_here

    def stored_index(place):
        blocks = lax.dynamic_slice_in_dim(stretch_order, place * stretches_here, stretches_here)
        local = jnp.arange(count_of_rows, dtype=jnp.int32)
        match = (local // block_rows)[:, None] == jnp.arange(stretches_here, dtype=jnp.int32)[None]
        return (
            jnp.sum(jnp.where(match, blocks[None, :], 0), axis=1) * block_rows + local % block_rows
        )

    key_index = jnp.concatenate([stored_index(block_source("ctx", step)) for step in range(ctx_size)])
    query_index = key_index[:count_of_rows]
    visible = key_index[None, :] <= query_index[:, None]

    float_tokens = all_tokens.astype(jnp.float32)
    inv_first_all = lax.rsqrt(
        jnp.mean(float_tokens * float_tokens, axis=1, keepdims=True) + EPSILON
    )
    first_normalized = (float_tokens * inv_first_all * full_gain).astype(jnp.bfloat16)
    flat_tokens = own_tokens.astype(jnp.float32)
    inv_first = inv_first_all[:local_rows]
    unit_first = flat_tokens * inv_first
    projected = plain_product(first_normalized, full_qkv)
    query = projected[:, :query_width]
    key = projected[:, query_width : query_width + kv_width]
    value_rows = projected[:, query_width + kv_width :].astype(jnp.bfloat16)
    query_scaled, query_unit, query_inv = per_head_norm(
        query.reshape(sequences, count_of_rows, query_heads_here, HEAD_SIZE), query_gain
    )
    key_scaled, key_unit, key_inv = per_head_norm(
        key.reshape(sequences, count_of_rows, kv_heads_here, HEAD_SIZE), key_norm_gain
    )
    query_heads = (
        apply_rotation(query_scaled, cosine_values, sine_values)
        .astype(jnp.bfloat16)
        .reshape(sequences, count_of_rows, kv_heads_here, grouped_heads, HEAD_SIZE)
    )
    key_rot = (
        apply_rotation(key_scaled, cosine_values, sine_values)
        .astype(jnp.bfloat16)
        .reshape(sequences, count_of_rows, kv_heads_here, HEAD_SIZE)
    )
    key_value = jnp.stack(
        [key_rot, value_rows.reshape(sequences, count_of_rows, kv_heads_here, HEAD_SIZE)]
    )
    all_key_value = jnp.concatenate(gather_blocks(key_value, "ctx"), axis=2)
    key_heads = all_key_value[0]
    value_heads = all_key_value[1]
    attended, log_total = attend(query_heads, key_heads, value_heads, visible)
    attended_flat = attended.reshape(total_rows, query_width)
    middle = flat_tokens + scatter_sum(
        split_rows(dot_right(attended_flat, full_output), members), "rep"
    )
    inv_second = lax.rsqrt(jnp.mean(middle * middle, axis=1, keepdims=True) + EPSILON)
    unit_second = middle * inv_second
    normed_own = (unit_second * full_ffn_gain).astype(jnp.bfloat16)
    normed_second = jnp.concatenate(gather_blocks(normed_own, "rep"), axis=0)
    gate_up = plain_product(normed_second, full_gate_up)
    gate_value = gate_up[:, :hidden_width]
    up_value = gate_up[:, hidden_width:]
    sigmoid_gate = jax.nn.sigmoid(gate_value)
    activated = gate_value * sigmoid_gate
    hidden = (activated * up_value).astype(jnp.bfloat16)
    hidden_grad = plain_product(all_grads, full_down)
    gate_grad = (
        hidden_grad * up_value * sigmoid_gate * (1.0 + gate_value * (1.0 - sigmoid_gate))
    ).astype(jnp.bfloat16)
    up_grad = (hidden_grad * activated).astype(jnp.bfloat16)
    gate_up_grad = jnp.concatenate([gate_grad, up_grad], axis=1)
    normed_grad_second = scatter_sum(
        split_rows(dot_right(gate_up_grad, full_gate_up), members), "rep"
    )
    block_sum = middle + scatter_sum(split_rows(dot_right(hidden, full_down), members), "rep")
    block_out = block_sum.astype(jnp.bfloat16).reshape(sequence_batch, count_of_rows, model_width)

    def owner_rows(left_sides, right_sides):
        columns = [
            dot_left(left_side, right_side).astype(jnp.bfloat16)
            for left_side, right_side in zip(left_sides, right_sides)
        ]
        return lax.psum_scatter(
            jnp.concatenate(columns, axis=1), owners, scatter_dimension=0, tiled=True
        )

    ffn_rows = owner_rows([normed_second, all_grads], [gate_up_grad, hidden])
    ffn_gain_part = jnp.sum(normed_grad_second * unit_second, axis=0)
    unit_grad_second = normed_grad_second * full_ffn_gain
    middle_grad = own_grads.astype(jnp.float32) + inv_second * (
        unit_grad_second
        - unit_second * jnp.mean(unit_grad_second * unit_second, axis=1, keepdims=True)
    )
    middle_grad_b = jnp.concatenate(
        gather_blocks(middle_grad.astype(jnp.bfloat16), "rep"), axis=0
    )
    attended_grad = (
        plain_product(middle_grad_b, full_output).astype(jnp.bfloat16).reshape(attended.shape)
    )
    query_rot_grad, key_terms, value_terms = attend_back(
        query_heads, key_heads, value_heads, attended, attended_grad, log_total, visible
    )
    own_terms = jnp.stack([key_terms, value_terms])
    key_value_grad = scatter_sum(
        [
            own_terms[:, :, place * count_of_rows : (place + 1) * count_of_rows]
            for place in range(ctx_size)
        ],
        "ctx",
    )
    query_gain_part, query_pre = per_head_norm_backward(
        reverse_rotation(
            query_rot_grad.reshape(sequences, count_of_rows, query_heads_here, HEAD_SIZE),
            cosine_values,
            sine_values,
        ),
        query_unit,
        query_inv,
        query_gain,
    )
    key_gain_part, key_pre = per_head_norm_backward(
        reverse_rotation(key_value_grad[0], cosine_values, sine_values),
        key_unit,
        key_inv,
        key_norm_gain,
    )
    projected_grad = jnp.concatenate(
        [
            query_pre.reshape(total_rows, query_width).astype(jnp.bfloat16),
            key_pre.reshape(total_rows, kv_width).astype(jnp.bfloat16),
            key_value_grad[1].reshape(total_rows, kv_width).astype(jnp.bfloat16),
        ],
        axis=1,
    )
    attn_rows = owner_rows([first_normalized, middle_grad_b], [projected_grad, attended_flat])
    normed_grad_first = scatter_sum(
        split_rows(dot_right(projected_grad, full_qkv), members), "rep"
    )
    attn_gain_part = jnp.sum(normed_grad_first * unit_first, axis=0)
    unit_grad_first = normed_grad_first * full_gain
    tokens_grad = middle_grad + inv_first * (
        unit_grad_first - unit_first * jnp.mean(unit_grad_first * unit_first, axis=1, keepdims=True)
    )
    gain_totals = lax.psum(
        (attn_gain_part, ffn_gain_part, query_gain_part, key_gain_part), ("rep",) + owners
    )
    attn_gain_grad = lax.dynamic_slice_in_dim(gain_totals[0], own_start, own_rows)
    ffn_gain_grad = lax.dynamic_slice_in_dim(gain_totals[1], own_start, own_rows)

    ffn_all = lax.all_gather(ffn_rows, "rep", axis=0)
    attn_all = lax.all_gather(attn_rows, "rep", axis=0)

    def whole(pieces, start, width):
        return jnp.concatenate(
            [pieces[place, :, start : start + width] for place in range(members)], axis=1
        ).astype(jnp.float32)

    return (
        block_out,
        tokens_grad.reshape(sequence_batch, count_of_rows, model_width),
        whole(attn_all, 0, query_width),
        whole(attn_all, query_width, kv_width),
        whole(attn_all, query_width + kv_width, kv_width),
        whole(attn_all, query_width + 2 * kv_width, query_width),
        whole(ffn_all, 0, hidden_width),
        whole(ffn_all, hidden_width, hidden_width),
        whole(ffn_all, 2 * hidden_width, hidden_width),
        attn_gain_grad,
        ffn_gain_grad,
        gain_totals[2],
        gain_totals[3],
    )


def solution(mesh):
    in_specs = (
        P(("rep", "shard"), "ctx", None),
        P(("rep", "shard"), "ctx", None),
        P(("rep", "shard"), "ctx"),
        P(),
        P(("shard", "ctx")),
        P(),
        P(),
        P(("shard", "ctx"), None),
        P(("shard", "ctx"), None),
        P(("shard", "ctx"), None),
        P(("shard", "ctx"), None),
        P(("shard", "ctx")),
        P(("shard", "ctx"), None),
        P(("shard", "ctx"), None),
        P(("shard", "ctx"), None),
    )
    out_specs = (
        P(("rep", "shard"), "ctx", None),
        P(("rep", "shard"), "ctx", None),
        P(("shard", "ctx"), None),
        P(("shard", "ctx"), None),
        P(("shard", "ctx"), None),
        P(("shard", "ctx"), None),
        P(("shard", "ctx"), None),
        P(("shard", "ctx"), None),
        P(("shard", "ctx"), None),
        P(("shard", "ctx")),
        P(("shard", "ctx")),
        P(),
        P(),
    )
    return jax.shard_map(
        per_device, mesh=mesh, in_specs=in_specs, out_specs=out_specs, check_vma=False
    )
```

```python
import math

import jax
import jax.numpy as jnp
from jax import lax
from jax.experimental import pallas as pl
from jax.experimental.pallas import tpu as pltpu
from jax.sharding import PartitionSpec as P

QUERY_HEADS = 16
KEY_VALUE_HEADS = 8
HEAD_SIZE = 128


EPSILON = 1e-06
ROPE_THETA = 1000000.0
NEGATIVE = -1e30
TEAM = ("rep", "ctx")
OWNERS = ("shard", "ctx")


def plain_product(left_side, right_side):
    return jnp.dot(left_side, right_side, preferred_element_type=jnp.float32)


def dot_right(left_side, right_side):
    return lax.dot_general(
        left_side, right_side, (((1,), (1,)), ((), ())), preferred_element_type=jnp.float32
    )


def dot_left(left_side, right_side):
    return lax.dot_general(
        left_side, right_side, (((0,), (0,)), ((), ())), preferred_element_type=jnp.float32
    )


def axis_bits(axis_name):
    size = lax.axis_size(axis_name)
    assert size & (size - 1) == 0
    return [(axis_name, 1 << place) for place in range(size.bit_length() - 1)]


def swap(value, step):
    axis_name, bit = step
    pairs = [(index, index ^ bit) for index in range(lax.axis_size(axis_name))]
    return lax.ppermute(value, axis_name, pairs)


def team_steps():
    return axis_bits("ctx") + axis_bits("rep")[::-1]


def gather_plain(value, steps):
    blocks = value[None]
    for step in steps:
        blocks = jnp.concatenate([blocks, swap(blocks, step)], axis=0)
    return blocks


def crossed(steps):
    return [steps[1], steps[0]] if len(steps) > 1 else list(steps)


def gather_rows(value):
    steps = team_steps()
    first, rest = steps[:2], steps[2:]
    front, back = jnp.split(value, 2, axis=0)
    front_blocks = gather_plain(front, crossed(first))
    back_blocks = gather_plain(back, first)
    if len(first) == 2:
        front_list = [front_blocks[place] for place in (0, 2, 1, 3)]
    else:
        front_list = list(front_blocks)
    back_list = list(back_blocks)
    for step in rest:
        near = [jnp.stack(front_list), jnp.stack(back_list)]
        far = [swap(blocks, step) for blocks in (front_blocks, back_blocks)]
        far_front = (
            [far[0][place] for place in (0, 2, 1, 3)] if len(front_list) == 4 else list(far[0])
        )
        front_list = front_list + far_front
        back_list = back_list + list(far[1])
        front_blocks, back_blocks = near
    pieces = []
    for front_piece, back_piece in zip(front_list, back_list):
        pieces += [front_piece, back_piece]
    return jnp.concatenate(pieces, axis=0)


def scatter_rows(value):
    steps = team_steps()
    first, rest = steps[:2], steps[2:]
    members = 1 << len(steps)
    rows = value.shape[0] // members
    halves = value.reshape(members, 2, rows // 2, value.shape[1])

    def shed(part, step):
        count = part.shape[0] // 2
        moved = swap(part[count:].astype(jnp.bfloat16), step)
        return part[:count] + moved.astype(jnp.float32)

    totals = []
    for half in range(2):
        part = halves[:, half]
        for step in rest[::-1]:
            part = shed(part, step)
        if half == 0 and len(first) == 2:
            moved = swap(part[1::2].astype(jnp.bfloat16), first[0])
            part = part[0::2] + moved.astype(jnp.float32)
            part = shed(part, first[1])
        else:
            for step in first[::-1]:
                part = shed(part, step)
        totals.append(part[0])
    return jnp.concatenate(totals, axis=0)


def everyone_sum(value):
    for axis_name in ("rep", "ctx", "shard"):
        for step in axis_bits(axis_name):
            value = value + swap(value, step)
    return value


def turned(values, cosine, sine):
    return values * cosine + pltpu.roll(values, HEAD_SIZE // 2, 1) * sine


def unit_rows(values):
    inverse = lax.rsqrt(jnp.mean(values * values, axis=-1, keepdims=True) + EPSILON)
    return (values * inverse, inverse)


def heads_of(projected_ref, cosine, sine, query_gain, key_gain, query_count):
    key_start = query_count * HEAD_SIZE
    queries = []
    for head in range(query_count):
        unit, inverse = unit_rows(projected_ref[:, head * HEAD_SIZE : (head + 1) * HEAD_SIZE])
        queries.append(
            (turned(unit * query_gain, cosine, sine).astype(jnp.bfloat16), unit, inverse)
        )
    key_unit, key_inverse = unit_rows(projected_ref[:, key_start : key_start + HEAD_SIZE])
    key_rot = turned(key_unit * key_gain, cosine, sine).astype(jnp.bfloat16)
    value_rows = projected_ref[:, key_start + HEAD_SIZE : key_start + 2 * HEAD_SIZE].astype(
        jnp.bfloat16
    )
    return queries, (key_rot, key_unit, key_inverse), value_rows


def probabilities(query_rot, key_rot, visible):
    scores = dot_right(query_rot, key_rot) * (1.0 / math.sqrt(HEAD_SIZE))
    scores = jnp.where(visible, scores, NEGATIVE)
    row_max = jnp.max(scores, axis=-1, keepdims=True)
    log_total = row_max + jnp.log(jnp.sum(jnp.exp(scores - row_max), axis=-1, keepdims=True))
    return jnp.exp(scores - log_total)


def attend_kernel(
    projected_ref, cosine_ref, sine_ref, row_ref, column_ref, query_gain_ref, key_gain_ref, out_ref
):
    query_count = out_ref.shape[1] // HEAD_SIZE
    visible = column_ref[...] <= row_ref[...]
    queries, (key_rot, _, _), value_rows = heads_of(
        projected_ref,
        cosine_ref[...],
        sine_ref[...],
        query_gain_ref[...],
        key_gain_ref[...],
        query_count,
    )
    for head in range(query_count):
        probs = probabilities(queries[head][0], key_rot, visible).astype(jnp.bfloat16)
        out_ref[:, head * HEAD_SIZE : (head + 1) * HEAD_SIZE] = plain_product(
            probs, value_rows
        ).astype(jnp.bfloat16)


def norm_back(gradient, unit, inverse, gain):
    gain_part = jnp.sum(gradient * unit, axis=0, keepdims=True)
    scaled = gradient * gain
    return (
        gain_part,
        inverse * (scaled - unit * jnp.mean(scaled * unit, axis=-1, keepdims=True)),
    )


def attend_back_kernel(
    projected_ref,
    attended_ref,
    attended_grad_ref,
    cosine_ref,
    sine_ref,
    row_ref,
    column_ref,
    query_gain_ref,
    key_gain_ref,
    out_ref,
    gain_ref,
):
    query_count = attended_ref.shape[1] // HEAD_SIZE
    key_start = query_count * HEAD_SIZE
    visible = column_ref[...] <= row_ref[...]
    cosine = cosine_ref[...]
    sine = sine_ref[...]
    scale = 1.0 / math.sqrt(HEAD_SIZE)
    queries, (key_rot, key_unit, key_inverse), value_rows = heads_of(
        projected_ref, cosine, sine, query_gain_ref[...], key_gain_ref[...], query_count
    )
    query_gain_part = jnp.zeros((1, HEAD_SIZE), jnp.float32)
    key_grad = jnp.zeros(key_unit.shape, jnp.float32)
    value_grad = jnp.zeros(key_unit.shape, jnp.float32)
    for head in range(query_count):
        columns = slice(head * HEAD_SIZE, (head + 1) * HEAD_SIZE)
        query_rot, query_unit, query_inverse = queries[head]
        grads = attended_grad_ref[:, columns]
        row_delta = jnp.sum(
            grads.astype(jnp.float32) * attended_ref[:, columns].astype(jnp.float32),
            axis=-1,
            keepdims=True,
        )
        prob_float = probabilities(query_rot, key_rot, visible)
        value_grad = value_grad + dot_left(prob_float.astype(jnp.bfloat16), grads)
        score_grad = (prob_float * (dot_right(grads, value_rows) - row_delta)).astype(jnp.bfloat16)
        query_grad = plain_product(score_grad, key_rot) * scale
        key_grad = key_grad + dot_left(score_grad, query_rot)
        part, query_pre = norm_back(
            turned(query_grad, cosine, -sine), query_unit, query_inverse, query_gain_ref[...]
        )
        query_gain_part = query_gain_part + part
        out_ref[:, columns] = query_pre.astype(jnp.bfloat16)
    key_gain_part, key_pre = norm_back(
        turned(key_grad * scale, cosine, -sine), key_unit, key_inverse, key_gain_ref[...]
    )
    out_ref[:, key_start : key_start + HEAD_SIZE] = key_pre.astype(jnp.bfloat16)
    out_ref[:, key_start + HEAD_SIZE : key_start + 2 * HEAD_SIZE] = value_grad.astype(jnp.bfloat16)

    @pl.when(pl.program_id(0) == 0)
    def _():
        gain_ref[...] = jnp.zeros_like(gain_ref)

    gain_ref[0:1, :] += query_gain_part
    gain_ref[1:2, :] += key_gain_part


def sequence_spec(rows, width):
    return pl.BlockSpec((rows, width), lambda place: (place, 0))


def fixed_spec(shape):
    return pl.BlockSpec(shape, lambda place: (0, 0))


def attention_call(kernel, out_specs, out_shape, wide, tables, small, rows):
    cosine, sine = tables
    return pl.pallas_call(
        kernel,
        grid=(wide[0].shape[0] // rows,),
        in_specs=[sequence_spec(rows, array.shape[1]) for array in wide]
        + [sequence_spec(rows, HEAD_SIZE)] * 2
        + [fixed_spec(array.shape) for array in small],
        out_specs=out_specs,
        out_shape=out_shape,
        compiler_params=pltpu.CompilerParams(dimension_semantics=("arbitrary",)),
    )(*wide, cosine, sine, *small)


def spread_kernel(place_ref, blocks_ref, *out_refs):
    start = 0
    for out_ref in out_refs:
        width = out_ref.shape[1]
        out_ref[...] = blocks_ref[0, :, start : start + width].astype(jnp.float32)
        start += width


def spread_columns(blocks, member, widths, order):
    count, rows, width = blocks.shape

    def source(place, member_ref):
        return (order(place ^ member_ref[0]), 0, 0)

    return pl.pallas_call(
        spread_kernel,
        grid_spec=pltpu.PrefetchScalarGridSpec(
            num_scalar_prefetch=1,
            grid=(count,),
            in_specs=[pl.BlockSpec((1, rows, width), source)],
            out_specs=[
                pl.BlockSpec((rows, size), lambda place, member_ref: (0, place)) for size in widths
            ],
        ),
        out_shape=[jax.ShapeDtypeStruct((rows, size * count), jnp.float32) for size in widths],
        compiler_params=pltpu.CompilerParams(dimension_semantics=("arbitrary",)),
    )(member.reshape(1), blocks)


def per_device(
    tokens,
    out_grad,
    positions,
    stretch_order,
    attn_gain,
    query_gain,
    key_norm_gain,
    query_weight,
    key_projection_matrix,
    value_projection_matrix,
    output_weight,
    ffn_gain,
    gate_weight,
    up_weight,
    down_weight,
):
    sequence_batch, count_of_rows, model_width = tokens.shape
    local_rows = sequence_batch * count_of_rows
    team = lax.axis_size(TEAM)
    ctx_size = lax.axis_size("ctx")
    ctx_place = lax.axis_index("ctx")
    member = lax.axis_index(TEAM)
    steps = team_steps()
    query_width = QUERY_HEADS // team * HEAD_SIZE
    kv_width = KEY_VALUE_HEADS // team * HEAD_SIZE
    hidden_width = gate_weight.shape[1] // team
    own_rows = model_width // lax.axis_size(OWNERS)
    own_start = lax.axis_index(OWNERS) * own_rows

    def ctx_columns(matrices, place):
        start_member = lax.axis_index("rep") * ctx_size + place
        pieces = []
        for matrix in matrices:
            width = matrix.shape[1] // team
            pieces.append(
                lax.dynamic_slice_in_dim(matrix, start_member * width, width, axis=1)
            )
        return jnp.concatenate(pieces, axis=1)

    def ctx_exchange(pick, axis):
        received = [pick(ctx_place)]
        for offset in range(1, ctx_size):
            pairs = [(index, index ^ offset) for index in range(ctx_size)]
            received.append(lax.ppermute(pick(ctx_place ^ offset), "ctx", pairs))
        if ctx_size == 1:
            return received[0]
        if ctx_size == 2:
            return jnp.where(
                ctx_place == 0,
                jnp.concatenate(received, axis=axis),
                jnp.concatenate(received[::-1], axis=axis),
            )
        stacked = jnp.stack(received)
        return jnp.concatenate(
            [
                lax.dynamic_index_in_dim(stacked, ctx_place ^ place, 0, keepdims=False)
                for place in range(ctx_size)
            ],
            axis=axis,
        )

    def team_weights(matrices):
        rows = ctx_exchange(lambda place: ctx_columns(matrices, place), 0)
        return lax.all_gather(rows, "shard", axis=0, tiled=True)

    attn_weights = team_weights(
        [query_weight, key_projection_matrix, value_projection_matrix, output_weight]
    )
    ffn_weights = team_weights([gate_weight, up_weight, down_weight])
    qkv_width = query_width + 2 * kv_width
    full_qkv = attn_weights[:, :qkv_width]
    full_output = attn_weights[:, qkv_width:]
    full_gate_up = ffn_weights[:, : 2 * hidden_width]
    full_down = ffn_weights[:, 2 * hidden_width :]
    gains = lax.all_gather(jnp.stack([attn_gain, ffn_gain]), OWNERS, axis=1, tiled=True).astype(
        jnp.float32
    )
    full_gain = gains[0][None, :]
    full_ffn_gain = gains[1][None, :]

    own_tokens = tokens.reshape(local_rows, model_width)
    own_grads = out_grad.reshape(local_rows, model_width)
    all_tokens = gather_rows(own_tokens)
    all_grads = gather_rows(own_grads)
    total_rows = all_tokens.shape[0]
    sequence_rows = count_of_rows * ctx_size
    assert sequence_batch == 1

    half_size = HEAD_SIZE // 2
    freq_steps = jnp.arange(HEAD_SIZE, dtype=jnp.int32)
    inverse = jnp.exp(
        (freq_steps % half_size).astype(jnp.float32) * (-2.0 * math.log(ROPE_THETA) / HEAD_SIZE)
    )
    all_positions = gather_plain(positions, steps).reshape(total_rows)
    angles = all_positions.astype(jnp.float32)[:, None] * inverse[None, :]
    tables = (
        jnp.cos(angles),
        jnp.sin(angles) * jnp.where(freq_steps < half_size, -1.0, 1.0)[None, :],
    )

    stretches_here = stretch_order.shape[0] // ctx_size
    block_rows = count_of_rows // stretches_here
    local = jnp.arange(count_of_rows, dtype=jnp.int32)
    match = (local // block_rows)[:, None] == jnp.arange(stretches_here, dtype=jnp.int32)[None]

    def stored_index(place):
        blocks = lax.dynamic_slice_in_dim(stretch_order, place * stretches_here, stretches_here)
        return (
            jnp.sum(jnp.where(match, blocks[None, :], 0), axis=1) * block_rows + local % block_rows
        )

    seq_index = jnp.concatenate([stored_index(ctx_place ^ offset) for offset in range(ctx_size)])
    small = (
        seq_index[:, None],
        seq_index[None, :],
        query_gain.astype(jnp.float32)[None, :],
        key_norm_gain.astype(jnp.float32)[None, :],
    )

    float_tokens = all_tokens.astype(jnp.float32)
    inv_first_all = lax.rsqrt(
        jnp.mean(float_tokens * float_tokens, axis=1, keepdims=True) + EPSILON
    )
    first_normalized = (float_tokens * inv_first_all * full_gain).astype(jnp.bfloat16)
    flat_tokens = own_tokens.astype(jnp.float32)
    inv_first = inv_first_all[:local_rows]
    unit_first = flat_tokens * inv_first
    projected = plain_product(first_normalized, full_qkv)
    attended = attention_call(
        attend_kernel,
        sequence_spec(sequence_rows, query_width),
        jax.ShapeDtypeStruct((total_rows, query_width), jnp.bfloat16),
        [projected],
        tables,
        small,
        sequence_rows,
    )
    middle = flat_tokens + scatter_rows(dot_right(attended, full_output))
    inv_second = lax.rsqrt(jnp.mean(middle * middle, axis=1, keepdims=True) + EPSILON)
    unit_second = middle * inv_second
    normed_second = gather_rows((unit_second * full_ffn_gain).astype(jnp.bfloat16))
    gate_up = plain_product(normed_second, full_gate_up)
    gate_value = gate_up[:, :hidden_width]
    up_value = gate_up[:, hidden_width:]
    sigmoid_gate = jax.nn.sigmoid(gate_value)
    activated = gate_value * sigmoid_gate
    hidden = (activated * up_value).astype(jnp.bfloat16)
    hidden_grad = plain_product(all_grads, full_down)
    gate_grad = (
        hidden_grad * up_value * sigmoid_gate * (1.0 + gate_value * (1.0 - sigmoid_gate))
    ).astype(jnp.bfloat16)
    up_grad = (hidden_grad * activated).astype(jnp.bfloat16)
    gate_up_grad = jnp.concatenate([gate_grad, up_grad], axis=1)

    def joined_products(pairs):
        return jnp.concatenate(
            [dot_left(left, right).astype(jnp.bfloat16) for left, right in pairs], axis=1
        )

    def shard_sum(rows):
        return lax.psum_scatter(rows, "shard", scatter_dimension=0, tiled=True)

    ffn_terms = joined_products([(normed_second, gate_up_grad), (all_grads, hidden)])
    ffn_terms, gate_up_grad = lax.optimization_barrier((ffn_terms, gate_up_grad))
    ffn_rows = shard_sum(ffn_terms)
    normed_grad_second = scatter_rows(dot_right(gate_up_grad, full_gate_up))
    ffn_gain_part = jnp.sum(normed_grad_second * unit_second, axis=0)
    unit_grad_second = normed_grad_second * full_ffn_gain
    middle_grad = own_grads.astype(jnp.float32) + inv_second * (
        unit_grad_second
        - unit_second * jnp.mean(unit_grad_second * unit_second, axis=1, keepdims=True)
    )
    middle_grad_b = gather_rows(middle_grad.astype(jnp.bfloat16))
    attended_grad = plain_product(middle_grad_b, full_output).astype(jnp.bfloat16)
    projected_grad, norm_gain_parts = attention_call(
        attend_back_kernel,
        [sequence_spec(sequence_rows, qkv_width), fixed_spec((8, HEAD_SIZE))],
        [
            jax.ShapeDtypeStruct((total_rows, qkv_width), jnp.bfloat16),
            jax.ShapeDtypeStruct((8, HEAD_SIZE), jnp.float32),
        ],
        [projected, attended, attended_grad],
        tables,
        small,
        sequence_rows,
    )
    attn_terms = joined_products([(first_normalized, projected_grad), (middle_grad_b, attended)])
    attn_terms, projected_grad = lax.optimization_barrier((attn_terms, projected_grad))
    attn_rows = shard_sum(attn_terms)
    block_sum = middle + scatter_rows(dot_right(hidden, full_down))
    block_out = block_sum.astype(jnp.bfloat16).reshape(sequence_batch, count_of_rows, model_width)
    normed_grad_first = scatter_rows(dot_right(projected_grad, full_qkv))
    attn_gain_part = jnp.sum(normed_grad_first * unit_first, axis=0)
    unit_grad_first = normed_grad_first * full_gain
    tokens_grad = middle_grad + inv_first * (
        unit_grad_first - unit_first * jnp.mean(unit_grad_first * unit_first, axis=1, keepdims=True)
    )
    gain_totals = everyone_sum(
        jnp.concatenate(
            [
                attn_gain_part.reshape(-1, HEAD_SIZE),
                ffn_gain_part.reshape(-1, HEAD_SIZE),
                norm_gain_parts,
            ],
            axis=0,
        )
    )
    gain_rows = model_width // HEAD_SIZE
    attn_gain_grad = lax.dynamic_slice_in_dim(
        gain_totals[:gain_rows].reshape(model_width), own_start, own_rows
    )
    ffn_gain_grad = lax.dynamic_slice_in_dim(
        gain_totals[gain_rows : 2 * gain_rows].reshape(model_width), own_start, own_rows
    )

    def block_order(offset):
        place = 0
        for position, (axis_name, bit) in enumerate(steps):
            weight = bit if axis_name == "ctx" else bit * ctx_size
            place = place + ((offset // weight) % 2) * (1 << position)
        return place

    def whole_columns(rows, widths):
        own = lax.dynamic_slice_in_dim(rows, ctx_place * own_rows, own_rows)
        blocks = [own]
        for offset in range(1, ctx_size):
            pairs = [(index, index ^ offset) for index in range(ctx_size)]
            sent = lax.dynamic_slice_in_dim(rows, (ctx_place ^ offset) * own_rows, own_rows)
            blocks.append(lax.ppermute(sent, "ctx", pairs))
        blocks = jnp.stack(blocks)
        for step in steps[len(axis_bits("ctx")) :]:
            blocks = jnp.concatenate([blocks, swap(blocks, step)], axis=0)
        return spread_columns(blocks, member, widths, block_order)

    gate_weight_grad, up_weight_grad, down_weight_grad = whole_columns(
        ffn_rows, [hidden_width] * 3
    )
    query_weight_grad, key_weight_grad, value_weight_grad, output_weight_grad = whole_columns(
        attn_rows, [query_width, kv_width, kv_width, query_width]
    )
    return (
        block_out,
        tokens_grad.reshape(sequence_batch, count_of_rows, model_width),
        query_weight_grad,
        key_weight_grad,
        value_weight_grad,
        output_weight_grad,
        gate_weight_grad,
        up_weight_grad,
        down_weight_grad,
        attn_gain_grad,
        ffn_gain_grad,
        gain_totals[2 * gain_rows],
        gain_totals[2 * gain_rows + 1],
    )


def solution(mesh):
    in_specs = (
        P(("rep", "shard"), "ctx", None),
        P(("rep", "shard"), "ctx", None),
        P(("rep", "shard"), "ctx"),
        P(),
        P(("shard", "ctx")),
        P(),
        P(),
        P(("shard", "ctx"), None),
        P(("shard", "ctx"), None),
        P(("shard", "ctx"), None),
        P(("shard", "ctx"), None),
        P(("shard", "ctx")),
        P(("shard", "ctx"), None),
        P(("shard", "ctx"), None),
        P(("shard", "ctx"), None),
    )
    out_specs = (
        P(("rep", "shard"), "ctx", None),
        P(("rep", "shard"), "ctx", None),
        P(("shard", "ctx"), None),
        P(("shard", "ctx"), None),
        P(("shard", "ctx"), None),
        P(("shard", "ctx"), None),
        P(("shard", "ctx"), None),
        P(("shard", "ctx"), None),
        P(("shard", "ctx"), None),
        P(("shard", "ctx")),
        P(("shard", "ctx")),
        P(),
        P(),
    )
    return jax.shard_map(
        per_device, mesh=mesh, in_specs=in_specs, out_specs=out_specs, check_vma=False
    )
```

```python
import functools
import math

import jax
import jax.numpy as jnp
from jax import lax
from jax.experimental import pallas as pl
from jax.experimental.pallas import tpu as pltpu
from jax.sharding import PartitionSpec as P

QUERY_HEADS = 16
KEY_VALUE_HEADS = 8
HEAD_SIZE = 128


EPSILON = 1e-06
ROPE_THETA = 1000000.0
NEGATIVE = -1e30
TEAM = ("rep", "ctx")
OWNERS = ("shard", "ctx")
FLOPS_HINT = 8_000_000_000


def plain_product(left_side, right_side):
    return jnp.dot(left_side, right_side, preferred_element_type=jnp.float32)


def dot_right(left_side, right_side):
    return lax.dot_general(
        left_side, right_side, (((1,), (1,)), ((), ())), preferred_element_type=jnp.float32
    )


def dot_left(left_side, right_side):
    return lax.dot_general(
        left_side, right_side, (((0,), (0,)), ((), ())), preferred_element_type=jnp.float32
    )


def axis_bits(axis_name):
    size = lax.axis_size(axis_name)
    assert size & (size - 1) == 0
    return [1 << place for place in range(size.bit_length() - 1)]


def swap(value, axes, offset):
    pairs = [(index, index ^ offset) for index in range(lax.axis_size(axes))]
    return lax.ppermute(value, axes, pairs)


def after(value, *others):
    return lax.optimization_barrier((value,) + others)[0]


def gather_plain(value, axes, offsets):
    blocks = value[None]
    for offset in offsets:
        blocks = jnp.concatenate([blocks, swap(blocks, axes, offset)], axis=0)
    return blocks


def team_layout():
    near = lax.axis_size("ctx")
    members = lax.axis_size(TEAM)
    direct = [offset for offset in range(members) if not offset & near]
    return near, direct, direct + [offset | near for offset in direct]


def gather_pieces(piece_for, *others):
    near, direct, _ = team_layout()
    pieces = [piece_for(0)]
    for offset in direct[:0:-1]:
        pieces.insert(1, swap(piece_for(offset), TEAM, offset))
    if others:
        pieces = [after(piece, *others) for piece in pieces]
    return pieces + [swap(piece, TEAM, near) for piece in pieces]


def near_sums(parts):
    keep, send_last, send_rest = parts
    near = team_layout()[0]
    last = swap(send_last, TEAM, near)
    rest = swap(send_rest, TEAM, near)
    split = send_rest.shape[0]
    return (
        keep[:split] + rest.astype(jnp.float32),
        keep[split:] + last.astype(jnp.float32),
    )


def direct_sums(sums):
    rest, last = sums
    _, direct, _ = team_layout()
    rows = last.shape[0]
    bands = [rest[place * rows : (place + 1) * rows] for place in range(len(direct) - 1)] + [last]
    total = bands[0]
    moved = [
        swap(part.astype(jnp.bfloat16), TEAM, offset)
        for offset, part in list(zip(direct, bands))[:0:-1]
    ]
    for part in moved:
        total = total + part.astype(jnp.float32)
    return total


def scatter_parts(value):
    rows = value.shape[0] // lax.axis_size(TEAM)
    half = value.shape[0] // 2
    sent = value[half:].astype(jnp.bfloat16)
    return value[:half], sent[half - rows :], sent[: half - rows]


def everyone_sum(value):
    for axis_name in ("rep", "ctx", "shard"):
        for bit in axis_bits(axis_name):
            value = value + swap(value, axis_name, bit)
    return value


def turned(values, cosine, sine):
    return values * cosine + pltpu.roll(values, HEAD_SIZE // 2, 1) * sine


def unit_rows(values):
    inverse = lax.rsqrt(jnp.mean(values * values, axis=-1, keepdims=True) + EPSILON)
    return (values * inverse, inverse)


def heads_of(projected_ref, cosine, sine, query_gain, key_gain, query_count):
    key_start = query_count * HEAD_SIZE
    queries = []
    for head in range(query_count):
        unit, inverse = unit_rows(projected_ref[:, head * HEAD_SIZE : (head + 1) * HEAD_SIZE])
        queries.append(
            (turned(unit * query_gain, cosine, sine).astype(jnp.bfloat16), unit, inverse)
        )
    key_unit, key_inverse = unit_rows(projected_ref[:, key_start : key_start + HEAD_SIZE])
    key_rot = turned(key_unit * key_gain, cosine, sine).astype(jnp.bfloat16)
    value_rows = projected_ref[:, key_start + HEAD_SIZE : key_start + 2 * HEAD_SIZE].astype(
        jnp.bfloat16
    )
    return queries, (key_rot, key_unit, key_inverse), value_rows


def probabilities(query_rot, key_rot, visible):
    scores = dot_right(query_rot, key_rot) * (1.0 / math.sqrt(HEAD_SIZE))
    scores = jnp.where(visible, scores, NEGATIVE)
    weights = jnp.exp(scores - jnp.max(scores, axis=-1, keepdims=True))
    return weights * (1.0 / jnp.sum(weights, axis=-1, keepdims=True))


def put_partial(value, first, keep_ref, last_ref, rest_ref):
    kept_rows, rest_rows = keep_ref.shape[0], rest_ref.shape[0]
    count = value.shape[0]
    if first < kept_rows:
        keep_ref[first : first + count, :] = value
        return
    start = first - kept_rows
    sent = value.astype(jnp.bfloat16)
    inside = max(0, min(count, rest_rows - start))
    if inside:
        rest_ref[start : start + inside, :] = sent[:inside]
    if inside < count:
        last_start = max(0, start - rest_rows)
        last_ref[last_start : last_start + count - inside, :] = sent[inside:]


def attend_kernel(
    normed_ref,
    cosine_ref,
    sine_ref,
    weights_ref,
    row_ref,
    column_ref,
    query_gain_ref,
    key_gain_ref,
    projected_ref,
    out_ref,
    keep_ref,
    last_ref,
    rest_ref,
):
    query_count = out_ref.shape[1] // HEAD_SIZE
    qkv_width = projected_ref.shape[1]
    length = row_ref.shape[0]
    visible = column_ref[...] <= row_ref[...]
    projected_ref[...] = plain_product(normed_ref[...], weights_ref[:, :qkv_width])
    for first in range(0, normed_ref.shape[0], length):
        rows = slice(first, first + length)
        queries, (key_rot, _, _), value_rows = heads_of(
            projected_ref.at[rows, :],
            cosine_ref[rows, :],
            sine_ref[rows, :],
            query_gain_ref[...],
            key_gain_ref[...],
            query_count,
        )
        for head in range(query_count):
            probs = probabilities(queries[head][0], key_rot, visible).astype(jnp.bfloat16)
            out_ref[rows, head * HEAD_SIZE : (head + 1) * HEAD_SIZE] = plain_product(
                probs, value_rows
            ).astype(jnp.bfloat16)
        put_partial(
            dot_right(out_ref[rows, :], weights_ref[:, qkv_width:]),
            first,
            keep_ref,
            last_ref,
            rest_ref,
        )


def feed_kernel(*refs):
    pieces = refs[:-8]
    (
        grads_ref,
        weights_ref,
        normed_ref,
        gate_up_grad_ref,
        hidden_ref,
        keep_ref,
        last_ref,
        rest_ref,
    ) = refs[-8:]
    hidden_width = hidden_ref.shape[1]
    height = pieces[0].shape[0]
    for place, piece in enumerate(pieces):
        normed_ref[place * height : (place + 1) * height, :] = piece[...]
    count = 2 * height
    for first in range(0, normed_ref.shape[0], count):
        rows = slice(first, first + count)
        gate_up = plain_product(normed_ref[rows, :], weights_ref[:, : 2 * hidden_width])
        gate_value = gate_up[:, :hidden_width]
        up_value = gate_up[:, hidden_width:]
        hidden_grad = plain_product(grads_ref[rows, :], weights_ref[:, 2 * hidden_width :])
        sigmoid_gate = jax.nn.sigmoid(gate_value)
        activated = gate_value * sigmoid_gate
        hidden_ref[rows, :] = (activated * up_value).astype(jnp.bfloat16)
        gate_up_grad_ref[rows, :hidden_width] = (
            hidden_grad * up_value * sigmoid_gate * (1.0 + gate_value * (1.0 - sigmoid_gate))
        ).astype(jnp.bfloat16)
        gate_up_grad_ref[rows, hidden_width:] = (hidden_grad * activated).astype(jnp.bfloat16)
        put_partial(
            dot_right(gate_up_grad_ref[rows, :], weights_ref[:, : 2 * hidden_width]),
            first,
            keep_ref,
            last_ref,
            rest_ref,
        )


def norm_back(gradient, unit, inverse, gain):
    gain_part = jnp.sum(gradient * unit, axis=0, keepdims=True)
    scaled = gradient * gain
    return (
        gain_part,
        inverse * (scaled - unit * jnp.mean(scaled * unit, axis=-1, keepdims=True)),
    )


def attend_back_kernel(*refs):
    pieces = refs[:-13]
    (
        projected_ref,
        attended_ref,
        cosine_ref,
        sine_ref,
        weights_ref,
        row_ref,
        column_ref,
        query_gain_ref,
        key_gain_ref,
        middle_grad_ref,
        out_ref,
        gain_ref,
        grads_ref,
    ) = refs[-13:]
    height = pieces[0].shape[0]
    qkv_width = projected_ref.shape[1]
    length = row_ref.shape[0]
    query_count = attended_ref.shape[1] // HEAD_SIZE
    key_start = query_count * HEAD_SIZE
    visible = column_ref[...] <= row_ref[...]
    scale = 1.0 / math.sqrt(HEAD_SIZE)
    for place, piece in enumerate(pieces):
        middle_grad_ref[place * height : (place + 1) * height, :] = piece[...]
    grads_ref[...] = plain_product(middle_grad_ref[...], weights_ref[:, qkv_width:]).astype(
        jnp.bfloat16
    )
    query_gain_part = jnp.zeros((1, HEAD_SIZE), jnp.float32)
    key_gain_part = jnp.zeros((1, HEAD_SIZE), jnp.float32)
    for first in range(0, projected_ref.shape[0], length):
        rows = slice(first, first + length)
        cosine = cosine_ref[rows, :]
        sine = sine_ref[rows, :]
        queries, (key_rot, key_unit, key_inverse), value_rows = heads_of(
            projected_ref.at[rows, :],
            cosine,
            sine,
            query_gain_ref[...],
            key_gain_ref[...],
            query_count,
        )
        key_grad = jnp.zeros(key_unit.shape, jnp.float32)
        value_grad = jnp.zeros(key_unit.shape, jnp.float32)
        for head in range(query_count):
            columns = slice(head * HEAD_SIZE, (head + 1) * HEAD_SIZE)
            query_rot, query_unit, query_inverse = queries[head]
            grads = grads_ref[rows, columns]
            row_delta = jnp.sum(
                grads.astype(jnp.float32) * attended_ref[rows, columns].astype(jnp.float32),
                axis=-1,
                keepdims=True,
            )
            prob_float = probabilities(query_rot, key_rot, visible)
            value_grad = value_grad + dot_left(prob_float.astype(jnp.bfloat16), grads)
            score_grad = (prob_float * (dot_right(grads, value_rows) - row_delta)).astype(
                jnp.bfloat16
            )
            query_grad = plain_product(score_grad, key_rot) * scale
            key_grad = key_grad + dot_left(score_grad, query_rot)
            part, query_pre = norm_back(
                turned(query_grad, cosine, -sine), query_unit, query_inverse, query_gain_ref[...]
            )
            query_gain_part = query_gain_part + part
            out_ref[rows, columns] = query_pre.astype(jnp.bfloat16)
        part, key_pre = norm_back(
            turned(key_grad * scale, cosine, -sine), key_unit, key_inverse, key_gain_ref[...]
        )
        key_gain_part = key_gain_part + part
        out_ref[rows, key_start : key_start + HEAD_SIZE] = key_pre.astype(jnp.bfloat16)
        out_ref[rows, key_start + HEAD_SIZE : key_start + 2 * HEAD_SIZE] = value_grad.astype(
            jnp.bfloat16
        )
    gain_ref[...] = jnp.zeros_like(gain_ref)
    gain_ref[0:1, :] = query_gain_part
    gain_ref[1:2, :] = key_gain_part


def whole_call(kernel, out_shapes, operands, scratch=(), flops=0):
    moved = sum(math.prod(shape) * jnp.dtype(kind).itemsize for shape, kind in out_shapes)
    moved += sum(array.size * array.dtype.itemsize for array in operands)
    return pl.pallas_call(
        kernel,
        in_specs=[pl.BlockSpec(memory_space=pltpu.VMEM)] * len(operands),
        out_specs=[pl.BlockSpec(memory_space=pltpu.VMEM)] * len(out_shapes),
        out_shape=[jax.ShapeDtypeStruct(shape, kind) for shape, kind in out_shapes],
        scratch_shapes=list(scratch),
        cost_estimate=pl.CostEstimate(flops=flops, transcendentals=0, bytes_accessed=moved),
    )(*operands)


def partial_shapes(rows, width, members):
    own = rows // members
    return [
        ((rows // 2, width), jnp.float32),
        ((own, width), jnp.bfloat16),
        ((rows // 2 - own, width), jnp.bfloat16),
    ]


def spread_kernel(member_ref, *refs, widths, offsets):
    blocks, out_refs = refs[: len(offsets)], refs[len(offsets) :]
    for block, offset in zip(blocks, offsets):
        place = member_ref[0] ^ offset
        start = 0
        for out_ref, width in zip(out_refs, widths):
            first = pl.multiple_of(place * width, width)
            out_ref[:, pl.ds(first, width)] = block[:, start : start + width].astype(jnp.float32)
            start += width


def spread_columns(blocks, member, widths):
    offsets = team_layout()[2]
    rows = blocks[0].shape[0]
    return pl.pallas_call(
        functools.partial(spread_kernel, widths=widths, offsets=offsets),
        in_specs=[pl.BlockSpec(memory_space=pltpu.SMEM)]
        + [pl.BlockSpec(memory_space=pltpu.VMEM)] * len(blocks),
        out_specs=[pl.BlockSpec(memory_space=pltpu.VMEM)] * len(widths),
        out_shape=[
            jax.ShapeDtypeStruct((rows, size * len(blocks)), jnp.float32) for size in widths
        ],
    )(member.reshape(1), *blocks)


def per_device(
    tokens,
    out_grad,
    positions,
    stretch_order,
    attn_gain,
    query_gain,
    key_norm_gain,
    query_weight,
    key_projection_matrix,
    value_projection_matrix,
    output_weight,
    ffn_gain,
    gate_weight,
    up_weight,
    down_weight,
):
    sequence_batch, count_of_rows, model_width = tokens.shape
    local_rows = sequence_batch * count_of_rows
    team = lax.axis_size(TEAM)
    ctx_size = lax.axis_size("ctx")
    ctx_place = lax.axis_index("ctx")
    member = lax.axis_index(TEAM)
    axis_offsets = [1 << bit for bit in range(team.bit_length() - 1)]
    query_width = QUERY_HEADS // team * HEAD_SIZE
    kv_width = KEY_VALUE_HEADS // team * HEAD_SIZE
    hidden_width = gate_weight.shape[1] // team
    own_rows = model_width // lax.axis_size(OWNERS)
    own_start = lax.axis_index(OWNERS) * own_rows

    def ctx_columns(matrices, place):
        start_member = lax.axis_index("rep") * ctx_size + place
        pieces = []
        for matrix in matrices:
            width = matrix.shape[1] // team
            pieces.append(
                lax.dynamic_slice_in_dim(matrix, start_member * width, width, axis=1)
            )
        return jnp.concatenate(pieces, axis=1)

    def ctx_exchange(pick, axis, *others):
        received = [pick(ctx_place)]
        for offset in range(1, ctx_size):
            received.append(swap(after(pick(ctx_place ^ offset), *others), "ctx", offset))
        if ctx_size == 1:
            return received[0]
        if ctx_size == 2:
            return jnp.where(
                ctx_place == 0,
                jnp.concatenate(received, axis=axis),
                jnp.concatenate(received[::-1], axis=axis),
            )
        stacked = jnp.stack(received)
        return jnp.concatenate(
            [
                lax.dynamic_index_in_dim(stacked, ctx_place ^ place, 0, keepdims=False)
                for place in range(ctx_size)
            ],
            axis=axis,
        )

    def team_rows(matrices, *others):
        return ctx_exchange(lambda place: ctx_columns(matrices, place), 0, *others)

    def all_rows(rows):
        return lax.all_gather(rows, "shard", axis=0, tiled=True)

    attn_part = team_rows(
        [query_weight, key_projection_matrix, value_projection_matrix, output_weight]
    )
    ffn_part = team_rows([gate_weight, up_weight, down_weight], attn_part)
    attn_weights = all_rows(attn_part)
    ffn_weights = all_rows(ffn_part)
    qkv_width = query_width + 2 * kv_width
    full_qkv = attn_weights[:, :qkv_width]
    full_down = ffn_weights[:, 2 * hidden_width :]
    owners = lax.axis_size(OWNERS)
    gain_blocks = gather_plain(
        jnp.stack([attn_gain, ffn_gain]),
        OWNERS, [1 << bit for bit in range(owners.bit_length() - 1)]
    )
    owner_places = jnp.arange(owners, dtype=jnp.int32)
    from_block = (owner_places[:, None] ^ lax.axis_index(OWNERS)) == owner_places[None, :]
    gains = jnp.einsum(
        "jk,kgf->gjf",
        from_block.astype(jnp.bfloat16),
        gain_blocks,
        preferred_element_type=jnp.float32,
    ).reshape(2, 1, model_width)
    full_gain = gains[0]
    full_ffn_gain = gains[1]

    own_tokens = tokens.reshape(local_rows, model_width)
    own_grads = out_grad.reshape(local_rows, model_width)
    token_source = after(own_tokens, attn_part)
    token_pieces = gather_pieces(lambda offset: token_source)
    all_tokens = jnp.concatenate(token_pieces, axis=0)
    grad_source = after(own_grads, *token_pieces)
    total_rows = all_tokens.shape[0]
    assert sequence_batch == 1

    half_size = HEAD_SIZE // 2
    freq_steps = jnp.arange(HEAD_SIZE, dtype=jnp.int32)
    inverse = jnp.exp(
        (freq_steps % half_size).astype(jnp.float32) * (-2.0 * math.log(ROPE_THETA) / HEAD_SIZE)
    )
    all_positions = gather_plain(
        after(positions, token_pieces[1]),
        TEAM,
        [bit for bit in axis_offsets if bit != ctx_size] + [ctx_size],
    ).reshape(total_rows)
    angles = all_positions.astype(jnp.float32)[:, None] * inverse[None, :]
    tables = (
        jnp.cos(angles),
        jnp.sin(angles) * jnp.where(freq_steps < half_size, -1.0, 1.0)[None, :],
    )

    stretches_here = stretch_order.shape[0] // ctx_size
    block_rows = count_of_rows // stretches_here
    local = jnp.arange(count_of_rows, dtype=jnp.int32)
    match = (local // block_rows)[:, None] == jnp.arange(stretches_here, dtype=jnp.int32)[None]

    def stored_index(place):
        blocks = lax.dynamic_slice_in_dim(stretch_order, place * stretches_here, stretches_here)
        return (
            jnp.sum(jnp.where(match, blocks[None, :], 0), axis=1) * block_rows + local % block_rows
        )

    seq_index = jnp.concatenate([stored_index(ctx_place ^ offset) for offset in range(ctx_size)])
    small = (
        seq_index[:, None],
        seq_index[None, :],
        query_gain.astype(jnp.float32)[None, :],
        key_norm_gain.astype(jnp.float32)[None, :],
    )

    float_tokens = all_tokens.astype(jnp.float32)
    inv_first_all = lax.rsqrt(
        jnp.mean(float_tokens * float_tokens, axis=1, keepdims=True) + EPSILON
    )
    unit_first_all = float_tokens * inv_first_all
    first_normalized = (unit_first_all * full_gain).astype(jnp.bfloat16)
    flat_tokens = own_tokens.astype(jnp.float32)
    inv_first = inv_first_all[:local_rows]
    unit_first = flat_tokens * inv_first
    bfloat = jnp.bfloat16
    projected, attended, *output_parts = whole_call(
        attend_kernel,
        [((total_rows, qkv_width), jnp.float32), ((total_rows, query_width), bfloat)]
        + partial_shapes(total_rows, model_width, team),
        [after(first_normalized, ffn_part), *tables, attn_weights, *small],
        flops=FLOPS_HINT,
    )
    grad_pieces = gather_pieces(lambda offset: grad_source, attended)
    all_grads = jnp.concatenate(grad_pieces, axis=0)
    middle = flat_tokens + direct_sums(near_sums(output_parts))
    inv_second = lax.rsqrt(jnp.mean(middle * middle, axis=1, keepdims=True) + EPSILON)
    unit_second = middle * inv_second
    normed_own = (unit_second * full_ffn_gain).astype(bfloat)
    normed_pieces = gather_pieces(lambda offset: normed_own)
    normed_second, gate_up_grad, hidden, *second_parts = whole_call(
        feed_kernel,
        [
            ((total_rows, model_width), bfloat),
            ((total_rows, 2 * hidden_width), bfloat),
            ((total_rows, hidden_width), bfloat),
        ]
        + partial_shapes(total_rows, model_width, team),
        [*normed_pieces, all_grads, ffn_weights],
        flops=FLOPS_HINT,
    )

    def joined_products(pairs):
        return jnp.concatenate(
            [dot_left(left, right).astype(jnp.bfloat16) for left, right in pairs], axis=1
        )

    def shard_sum(rows):
        return lax.psum_scatter(rows, "shard", scatter_dimension=0, tiled=True)

    second_sums = near_sums(second_parts)
    ffn_terms = joined_products(
        [(normed_second, after(gate_up_grad, *second_sums)), (all_grads, hidden)]
    )
    ffn_rows = shard_sum(ffn_terms)
    normed_grad_second = after(direct_sums(second_sums), ffn_terms)
    ffn_gain_part = jnp.sum(normed_grad_second * unit_second, axis=0)
    unit_grad_second = normed_grad_second * full_ffn_gain
    middle_grad = own_grads.astype(jnp.float32) + inv_second * (
        unit_grad_second
        - unit_second * jnp.mean(unit_grad_second * unit_second, axis=1, keepdims=True)
    )
    grad_own = middle_grad.astype(bfloat)
    middle_pieces = gather_pieces(lambda offset: grad_own)
    down_partial = dot_right(after(hidden, grad_own), full_down)
    down_parts = scatter_parts(down_partial)
    down_sums = near_sums(down_parts)
    middle_grad_b, projected_grad, norm_gain_parts = whole_call(
        attend_back_kernel,
        [
            ((total_rows, model_width), bfloat),
            ((total_rows, qkv_width), bfloat),
            ((8, HEAD_SIZE), jnp.float32),
        ],
        [
            *middle_pieces[:-1],
            after(middle_pieces[-1], *down_sums),
            projected,
            attended,
            *tables,
            attn_weights,
            *small,
        ],
        [pltpu.VMEM((total_rows, query_width), bfloat)],
        flops=FLOPS_HINT,
    )
    block_sum = middle + direct_sums(down_sums)
    block_out = block_sum.astype(bfloat).reshape(sequence_batch, count_of_rows, model_width)

    def rows_for(rows):
        return lambda offset: lax.dynamic_slice_in_dim(
            rows, (ctx_place ^ (offset % ctx_size)) * own_rows, own_rows
        )

    projected_grad = after(projected_grad, ffn_rows)
    ffn_pieces = gather_pieces(rows_for(ffn_rows))
    attn_terms = joined_products([(first_normalized, projected_grad), (middle_grad_b, attended)])
    attn_rows = shard_sum(attn_terms)
    first_partial = dot_right(after(projected_grad, attn_terms), full_qkv)
    attn_gain_part = jnp.sum(first_partial * unit_first_all, axis=0)
    normed_grad_first = direct_sums(near_sums(scatter_parts(first_partial)))
    unit_grad_first = normed_grad_first * full_gain
    tokens_grad = middle_grad + inv_first * (
        unit_grad_first - unit_first * jnp.mean(unit_grad_first * unit_first, axis=1, keepdims=True)
    )
    gain_totals = everyone_sum(
        jnp.concatenate(
            [
                attn_gain_part.reshape(-1, HEAD_SIZE),
                ffn_gain_part.reshape(-1, HEAD_SIZE),
                norm_gain_parts,
            ],
            axis=0,
        )
    )
    gain_rows = model_width // HEAD_SIZE
    attn_gain_grad = lax.dynamic_slice_in_dim(
        gain_totals[:gain_rows].reshape(model_width), own_start, own_rows
    )
    ffn_gain_grad = lax.dynamic_slice_in_dim(
        gain_totals[gain_rows : 2 * gain_rows].reshape(model_width), own_start, own_rows
    )

    ffn_outs = spread_columns(ffn_pieces, member, [hidden_width] * 3)
    gate_weight_grad, up_weight_grad, down_weight_grad = ffn_outs
    attn_rows = after(attn_rows, *ffn_outs, tokens_grad, gain_totals, block_out)
    query_weight_grad, key_weight_grad, value_weight_grad, output_weight_grad = spread_columns(
        gather_pieces(rows_for(attn_rows)),
        member,
        [query_width, kv_width, kv_width, query_width],
    )
    return (
        block_out,
        tokens_grad.reshape(sequence_batch, count_of_rows, model_width),
        query_weight_grad,
        key_weight_grad,
        value_weight_grad,
        output_weight_grad,
        gate_weight_grad,
        up_weight_grad,
        down_weight_grad,
        attn_gain_grad,
        ffn_gain_grad,
        gain_totals[2 * gain_rows],
        gain_totals[2 * gain_rows + 1],
    )


def solution(mesh):
    in_specs = (
        P(("rep", "shard"), "ctx", None),
        P(("rep", "shard"), "ctx", None),
        P(("rep", "shard"), "ctx"),
        P(),
        P(("shard", "ctx")),
        P(),
        P(),
        P(("shard", "ctx"), None),
        P(("shard", "ctx"), None),
        P(("shard", "ctx"), None),
        P(("shard", "ctx"), None),
        P(("shard", "ctx")),
        P(("shard", "ctx"), None),
        P(("shard", "ctx"), None),
        P(("shard", "ctx"), None),
    )
    out_specs = (
        P(("rep", "shard"), "ctx", None),
        P(("rep", "shard"), "ctx", None),
        P(("shard", "ctx"), None),
        P(("shard", "ctx"), None),
        P(("shard", "ctx"), None),
        P(("shard", "ctx"), None),
        P(("shard", "ctx"), None),
        P(("shard", "ctx"), None),
        P(("shard", "ctx"), None),
        P(("shard", "ctx")),
        P(("shard", "ctx")),
        P(),
        P(),
    )

    return jax.shard_map(
        per_device, mesh=mesh, in_specs=in_specs, out_specs=out_specs, check_vma=False
    )
```

```python
import functools
import math

import jax
import jax.numpy as jnp
from jax import lax
from jax.experimental import pallas as pl
from jax.experimental.pallas import tpu as pltpu
from jax.sharding import PartitionSpec as P

QUERY_HEADS = 16
KEY_VALUE_HEADS = 8
HEAD_SIZE = 128


EPSILON = 1e-06
ROPE_THETA = 1000000.0
NEGATIVE = -1e30
TEAM = ("rep", "ctx")
OWNERS = ("shard", "ctx")
FLOPS_HINT = 8_000_000_000


def plain_product(left_side, right_side):
    return jnp.dot(left_side, right_side, preferred_element_type=jnp.float32)


def dot_right(left_side, right_side):
    return lax.dot_general(
        left_side, right_side, (((1,), (1,)), ((), ())), preferred_element_type=jnp.float32
    )


def dot_left(left_side, right_side):
    return lax.dot_general(
        left_side, right_side, (((0,), (0,)), ((), ())), preferred_element_type=jnp.float32
    )


def axis_bits(axis_name):
    size = lax.axis_size(axis_name)
    assert size & (size - 1) == 0
    return [1 << place for place in range(size.bit_length() - 1)]


def swap(value, axes, offset):
    pairs = [(index, index ^ offset) for index in range(lax.axis_size(axes))]
    return lax.ppermute(value, axes, pairs)


def after(value, *others):
    return lax.optimization_barrier((value,) + others)[0]


def gather_plain(value, axes, offsets):
    blocks = value[None]
    for offset in offsets:
        blocks = jnp.concatenate([blocks, swap(blocks, axes, offset)], axis=0)
    return blocks


def team_layout():
    near = lax.axis_size("ctx")
    members = lax.axis_size(TEAM)
    direct = [offset for offset in range(members) if not offset & near]
    return near, direct, direct + [offset | near for offset in direct]


def gather_pieces(piece_for, *others):
    near, direct, _ = team_layout()
    pieces = [piece_for(0)]
    for offset in direct[:0:-1]:
        pieces.insert(1, swap(piece_for(offset), TEAM, offset))
    if others:
        pieces = [after(piece, *others) for piece in pieces]
    return pieces + [swap(piece, TEAM, near) for piece in pieces]


def near_sums(parts):
    keep, send_last, send_rest = parts
    near = team_layout()[0]
    last = swap(send_last, TEAM, near)
    rest = swap(send_rest, TEAM, near)
    split = send_rest.shape[0]
    return (
        keep[:split] + rest.astype(jnp.float32),
        keep[split:] + last.astype(jnp.float32),
    )


def direct_sums(sums, sent=None):
    rest, last = sent or [part.astype(jnp.bfloat16) for part in sums]
    _, direct, _ = team_layout()
    rows = last.shape[0]
    bands = [rest[place * rows : (place + 1) * rows] for place in range(len(direct) - 1)] + [last]
    total = sums[0][:rows]
    moved = [
        swap(part, TEAM, offset) for offset, part in list(zip(direct, bands))[:0:-1]
    ]
    for part in moved:
        total = total + part.astype(jnp.float32)
    return total


def scatter_parts(value):
    rows = value.shape[0] // lax.axis_size(TEAM)
    half = value.shape[0] // 2
    sent = value[half:].astype(jnp.bfloat16)
    return value[:half], sent[half - rows :], sent[: half - rows]


def everyone_sum(value):
    for axis_name in ("shard", "rep", "ctx"):
        size = lax.axis_size(axis_name)
        if size <= 4:
            moved = [swap(value, axis_name, offset) for offset in range(1, size)]
            value = sum(moved, value)
        else:
            for bit in axis_bits(axis_name):
                value = value + swap(value, axis_name, bit)
    return value


def turned(values, cosine, sine):
    return values * cosine + pltpu.roll(values, HEAD_SIZE // 2, 1) * sine


def unit_rows(values):
    inverse = lax.rsqrt(jnp.mean(values * values, axis=-1, keepdims=True) + EPSILON)
    return (values * inverse, inverse)


def heads_of(projected_ref, cosine, sine, query_gain, key_gain, query_count):
    key_start = query_count * HEAD_SIZE
    queries = []
    for head in range(query_count):
        unit, inverse = unit_rows(projected_ref[:, head * HEAD_SIZE : (head + 1) * HEAD_SIZE])
        queries.append(
            (turned(unit * query_gain, cosine, sine).astype(jnp.bfloat16), unit, inverse)
        )
    key_unit, key_inverse = unit_rows(projected_ref[:, key_start : key_start + HEAD_SIZE])
    key_rot = turned(key_unit * key_gain, cosine, sine).astype(jnp.bfloat16)
    value_rows = projected_ref[:, key_start + HEAD_SIZE : key_start + 2 * HEAD_SIZE].astype(
        jnp.bfloat16
    )
    return queries, (key_rot, key_unit, key_inverse), value_rows


def probabilities(query_rot, key_rot, visible):
    scores = dot_right(query_rot, key_rot) * (1.0 / math.sqrt(HEAD_SIZE))
    scores = jnp.where(visible, scores, NEGATIVE)
    weights = jnp.exp(scores - jnp.max(scores, axis=-1, keepdims=True))
    return weights * (1.0 / jnp.sum(weights, axis=-1, keepdims=True))


def put_partial(value, first, keep_ref, last_ref, rest_ref):
    kept_rows, rest_rows = keep_ref.shape[0], rest_ref.shape[0]
    count = value.shape[0]
    if first < kept_rows:
        keep_ref[first : first + count, :] = value
        return
    start = first - kept_rows
    sent = value.astype(jnp.bfloat16)
    inside = max(0, min(count, rest_rows - start))
    if inside:
        rest_ref[start : start + inside, :] = sent[:inside]
    if inside < count:
        last_start = max(0, start - rest_rows)
        last_ref[last_start : last_start + count - inside, :] = sent[inside:]


def attend_kernel(
    normed_ref,
    cosine_ref,
    sine_ref,
    weights_ref,
    row_ref,
    column_ref,
    query_gain_ref,
    key_gain_ref,
    projected_ref,
    out_ref,
    keep_ref,
    last_ref,
    rest_ref,
):
    query_count = out_ref.shape[1] // HEAD_SIZE
    qkv_width = projected_ref.shape[1]
    length = row_ref.shape[0]
    visible = column_ref[...] <= row_ref[...]
    projected_ref[...] = plain_product(normed_ref[...], weights_ref[:, :qkv_width])
    for first in range(0, normed_ref.shape[0], length):
        rows = slice(first, first + length)
        queries, (key_rot, _, _), value_rows = heads_of(
            projected_ref.at[rows, :],
            cosine_ref[rows, :],
            sine_ref[rows, :],
            query_gain_ref[...],
            key_gain_ref[...],
            query_count,
        )
        for head in range(query_count):
            probs = probabilities(queries[head][0], key_rot, visible).astype(jnp.bfloat16)
            out_ref[rows, head * HEAD_SIZE : (head + 1) * HEAD_SIZE] = plain_product(
                probs, value_rows
            ).astype(jnp.bfloat16)
        put_partial(
            dot_right(out_ref[rows, :], weights_ref[:, qkv_width:]),
            first,
            keep_ref,
            last_ref,
            rest_ref,
        )


def feed_kernel(*refs):
    pieces = refs[:-11]
    (
        grads_ref,
        weights_ref,
        normed_ref,
        gate_up_grad_ref,
        hidden_ref,
        keep_ref,
        last_ref,
        rest_ref,
        down_keep_ref,
        down_last_ref,
        down_rest_ref,
    ) = refs[-11:]
    hidden_width = hidden_ref.shape[1]
    height = pieces[0].shape[0]
    for place, piece in enumerate(pieces):
        normed_ref[place * height : (place + 1) * height, :] = piece[...]
    count = 2 * height
    for first in range(0, normed_ref.shape[0], count):
        rows = slice(first, first + count)
        gate_up = plain_product(normed_ref[rows, :], weights_ref[:, : 2 * hidden_width])
        gate_value = gate_up[:, :hidden_width]
        up_value = gate_up[:, hidden_width:]
        hidden_grad = plain_product(grads_ref[rows, :], weights_ref[:, 2 * hidden_width :])
        sigmoid_gate = jax.nn.sigmoid(gate_value)
        activated = gate_value * sigmoid_gate
        hidden_ref[rows, :] = (activated * up_value).astype(jnp.bfloat16)
        gate_up_grad_ref[rows, :hidden_width] = (
            hidden_grad * up_value * sigmoid_gate * (1.0 + gate_value * (1.0 - sigmoid_gate))
        ).astype(jnp.bfloat16)
        gate_up_grad_ref[rows, hidden_width:] = (hidden_grad * activated).astype(jnp.bfloat16)
        put_partial(
            dot_right(gate_up_grad_ref[rows, :], weights_ref[:, : 2 * hidden_width]),
            first,
            keep_ref,
            last_ref,
            rest_ref,
        )
        put_partial(
            dot_right(hidden_ref[rows, :], weights_ref[:, 2 * hidden_width :]),
            first,
            down_keep_ref,
            down_last_ref,
            down_rest_ref,
        )


def norm_back(gradient, unit, inverse, gain):
    gain_part = jnp.sum(gradient * unit, axis=0, keepdims=True)
    scaled = gradient * gain
    return (
        gain_part,
        inverse * (scaled - unit * jnp.mean(scaled * unit, axis=-1, keepdims=True)),
    )


def attend_back_kernel(*refs):
    pieces = refs[:-13]
    (
        projected_ref,
        attended_ref,
        cosine_ref,
        sine_ref,
        weights_ref,
        row_ref,
        column_ref,
        query_gain_ref,
        key_gain_ref,
        middle_grad_ref,
        out_ref,
        gain_ref,
        grads_ref,
    ) = refs[-13:]
    height = pieces[0].shape[0]
    qkv_width = projected_ref.shape[1]
    length = row_ref.shape[0]
    query_count = attended_ref.shape[1] // HEAD_SIZE
    key_start = query_count * HEAD_SIZE
    visible = column_ref[...] <= row_ref[...]
    scale = 1.0 / math.sqrt(HEAD_SIZE)
    for place, piece in enumerate(pieces):
        middle_grad_ref[place * height : (place + 1) * height, :] = piece[...]
    grads_ref[...] = plain_product(middle_grad_ref[...], weights_ref[:, qkv_width:]).astype(
        jnp.bfloat16
    )
    query_gain_part = jnp.zeros((1, HEAD_SIZE), jnp.float32)
    key_gain_part = jnp.zeros((1, HEAD_SIZE), jnp.float32)
    for first in range(0, projected_ref.shape[0], length):
        rows = slice(first, first + length)
        cosine = cosine_ref[rows, :]
        sine = sine_ref[rows, :]
        queries, (key_rot, key_unit, key_inverse), value_rows = heads_of(
            projected_ref.at[rows, :],
            cosine,
            sine,
            query_gain_ref[...],
            key_gain_ref[...],
            query_count,
        )
        key_grad = jnp.zeros(key_unit.shape, jnp.float32)
        value_grad = jnp.zeros(key_unit.shape, jnp.float32)
        for head in range(query_count):
            columns = slice(head * HEAD_SIZE, (head + 1) * HEAD_SIZE)
            query_rot, query_unit, query_inverse = queries[head]
            grads = grads_ref[rows, columns]
            row_delta = jnp.sum(
                grads.astype(jnp.float32) * attended_ref[rows, columns].astype(jnp.float32),
                axis=-1,
                keepdims=True,
            )
            prob_float = probabilities(query_rot, key_rot, visible)
            value_grad = value_grad + dot_left(prob_float.astype(jnp.bfloat16), grads)
            score_grad = (prob_float * (dot_right(grads, value_rows) - row_delta)).astype(
                jnp.bfloat16
            )
            query_grad = plain_product(score_grad, key_rot) * scale
            key_grad = key_grad + dot_left(score_grad, query_rot)
            part, query_pre = norm_back(
                turned(query_grad, cosine, -sine), query_unit, query_inverse, query_gain_ref[...]
            )
            query_gain_part = query_gain_part + part
            out_ref[rows, columns] = query_pre.astype(jnp.bfloat16)
        part, key_pre = norm_back(
            turned(key_grad * scale, cosine, -sine), key_unit, key_inverse, key_gain_ref[...]
        )
        key_gain_part = key_gain_part + part
        out_ref[rows, key_start : key_start + HEAD_SIZE] = key_pre.astype(jnp.bfloat16)
        out_ref[rows, key_start + HEAD_SIZE : key_start + 2 * HEAD_SIZE] = value_grad.astype(
            jnp.bfloat16
        )
    gain_ref[...] = jnp.zeros_like(gain_ref)
    gain_ref[0:1, :] = query_gain_part
    gain_ref[1:2, :] = key_gain_part


def whole_call(kernel, out_shapes, operands, scratch=(), flops=0):
    moved = sum(math.prod(shape) * jnp.dtype(kind).itemsize for shape, kind in out_shapes)
    moved += sum(array.size * array.dtype.itemsize for array in operands)
    return pl.pallas_call(
        kernel,
        in_specs=[pl.BlockSpec(memory_space=pltpu.VMEM)] * len(operands),
        out_specs=[pl.BlockSpec(memory_space=pltpu.VMEM)] * len(out_shapes),
        out_shape=[jax.ShapeDtypeStruct(shape, kind) for shape, kind in out_shapes],
        scratch_shapes=list(scratch),
        cost_estimate=pl.CostEstimate(flops=flops, transcendentals=0, bytes_accessed=moved),
    )(*operands)


def partial_shapes(rows, width, members):
    own = rows // members
    return [
        ((rows // 2, width), jnp.float32),
        ((own, width), jnp.bfloat16),
        ((rows // 2 - own, width), jnp.bfloat16),
    ]


def spread_kernel(member_ref, *refs, widths, offsets):
    blocks, out_refs = refs[: len(offsets)], refs[len(offsets) :]
    for block, offset in zip(blocks, offsets):
        place = member_ref[0] ^ offset
        start = 0
        for out_ref, width in zip(out_refs, widths):
            first = pl.multiple_of(place * width, width)
            out_ref[:, pl.ds(first, width)] = block[:, start : start + width].astype(jnp.float32)
            start += width


def spread_columns(blocks, member, widths):
    offsets = team_layout()[2]
    rows = blocks[0].shape[0]
    return pl.pallas_call(
        functools.partial(spread_kernel, widths=widths, offsets=offsets),
        in_specs=[pl.BlockSpec(memory_space=pltpu.SMEM)]
        + [pl.BlockSpec(memory_space=pltpu.VMEM)] * len(blocks),
        out_specs=[pl.BlockSpec(memory_space=pltpu.VMEM)] * len(widths),
        out_shape=[
            jax.ShapeDtypeStruct((rows, size * len(blocks)), jnp.float32) for size in widths
        ],
    )(member.reshape(1), *blocks)


def per_device(
    tokens,
    out_grad,
    positions,
    stretch_order,
    attn_gain,
    query_gain,
    key_norm_gain,
    query_weight,
    key_projection_matrix,
    value_projection_matrix,
    output_weight,
    ffn_gain,
    gate_weight,
    up_weight,
    down_weight,
):
    sequence_batch, count_of_rows, model_width = tokens.shape
    local_rows = sequence_batch * count_of_rows
    team = lax.axis_size(TEAM)
    ctx_size = lax.axis_size("ctx")
    ctx_place = lax.axis_index("ctx")
    member = lax.axis_index(TEAM)
    axis_offsets = [1 << bit for bit in range(team.bit_length() - 1)]
    query_width = QUERY_HEADS // team * HEAD_SIZE
    kv_width = KEY_VALUE_HEADS // team * HEAD_SIZE
    hidden_width = gate_weight.shape[1] // team
    own_rows = model_width // lax.axis_size(OWNERS)
    own_start = lax.axis_index(OWNERS) * own_rows

    def ctx_columns(matrices, place):
        start_member = lax.axis_index("rep") * ctx_size + place
        pieces = []
        for matrix in matrices:
            width = matrix.shape[1] // team
            pieces.append(
                lax.dynamic_slice_in_dim(matrix, start_member * width, width, axis=1)
            )
        return jnp.concatenate(pieces, axis=1)

    def ctx_exchange(pick, axis, *others):
        received = [pick(ctx_place)]
        for offset in range(1, ctx_size):
            received.append(swap(after(pick(ctx_place ^ offset), *others), "ctx", offset))
        if ctx_size == 1:
            return received[0]
        if ctx_size == 2:
            return jnp.where(
                ctx_place == 0,
                jnp.concatenate(received, axis=axis),
                jnp.concatenate(received[::-1], axis=axis),
            )
        stacked = jnp.stack(received)
        return jnp.concatenate(
            [
                lax.dynamic_index_in_dim(stacked, ctx_place ^ place, 0, keepdims=False)
                for place in range(ctx_size)
            ],
            axis=axis,
        )

    def team_rows(matrices, *others):
        return ctx_exchange(lambda place: ctx_columns(matrices, place), 0, *others)

    def all_rows(rows):
        return lax.all_gather(rows, "shard", axis=0, tiled=True)

    attn_part = team_rows(
        [query_weight, key_projection_matrix, value_projection_matrix, output_weight]
    )
    ffn_part = team_rows([gate_weight, up_weight, down_weight], attn_part)
    attn_weights = all_rows(attn_part)
    ffn_weights = all_rows(ffn_part)
    qkv_width = query_width + 2 * kv_width
    full_qkv = attn_weights[:, :qkv_width]
    owners = lax.axis_size(OWNERS)
    gain_blocks = gather_plain(
        jnp.stack([attn_gain, ffn_gain]),
        OWNERS, [1 << bit for bit in range(owners.bit_length() - 1)]
    )
    owner_places = jnp.arange(owners, dtype=jnp.int32)
    from_block = (owner_places[:, None] ^ lax.axis_index(OWNERS)) == owner_places[None, :]
    gains = jnp.einsum(
        "jk,kgf->gjf",
        from_block.astype(jnp.bfloat16),
        gain_blocks,
        preferred_element_type=jnp.float32,
    ).reshape(2, 1, model_width)
    full_gain = gains[0]
    full_ffn_gain = gains[1]

    own_tokens = tokens.reshape(local_rows, model_width)
    own_grads = out_grad.reshape(local_rows, model_width)
    token_source = after(own_tokens, attn_part)
    token_pieces = gather_pieces(lambda offset: token_source)
    all_tokens = jnp.concatenate(token_pieces, axis=0)
    grad_source = after(own_grads, *token_pieces)
    total_rows = all_tokens.shape[0]
    assert sequence_batch == 1

    half_size = HEAD_SIZE // 2
    freq_steps = jnp.arange(HEAD_SIZE, dtype=jnp.int32)
    inverse = jnp.exp(
        (freq_steps % half_size).astype(jnp.float32) * (-2.0 * math.log(ROPE_THETA) / HEAD_SIZE)
    )
    all_positions = gather_plain(
        after(positions, token_pieces[1]),
        TEAM,
        [bit for bit in axis_offsets if bit != ctx_size] + [ctx_size],
    ).reshape(total_rows)
    angles = all_positions.astype(jnp.float32)[:, None] * inverse[None, :]
    tables = (
        jnp.cos(angles),
        jnp.sin(angles) * jnp.where(freq_steps < half_size, -1.0, 1.0)[None, :],
    )

    stretches_here = stretch_order.shape[0] // ctx_size
    block_rows = count_of_rows // stretches_here
    local = jnp.arange(count_of_rows, dtype=jnp.int32)
    match = (local // block_rows)[:, None] == jnp.arange(stretches_here, dtype=jnp.int32)[None]

    def stored_index(place):
        blocks = lax.dynamic_slice_in_dim(stretch_order, place * stretches_here, stretches_here)
        return (
            jnp.sum(jnp.where(match, blocks[None, :], 0), axis=1) * block_rows + local % block_rows
        )

    seq_index = jnp.concatenate([stored_index(ctx_place ^ offset) for offset in range(ctx_size)])
    small = (
        seq_index[:, None],
        seq_index[None, :],
        query_gain.astype(jnp.float32)[None, :],
        key_norm_gain.astype(jnp.float32)[None, :],
    )

    float_tokens = all_tokens.astype(jnp.float32)
    inv_first_all = lax.rsqrt(
        jnp.mean(float_tokens * float_tokens, axis=1, keepdims=True) + EPSILON
    )
    unit_first_all = float_tokens * inv_first_all
    first_normalized = (unit_first_all * full_gain).astype(jnp.bfloat16)
    flat_tokens = own_tokens.astype(jnp.float32)
    inv_first = inv_first_all[:local_rows]
    unit_first = flat_tokens * inv_first
    bfloat = jnp.bfloat16
    projected, attended, *output_parts = whole_call(
        attend_kernel,
        [((total_rows, qkv_width), jnp.float32), ((total_rows, query_width), bfloat)]
        + partial_shapes(total_rows, model_width, team),
        [after(first_normalized, ffn_part), *tables, attn_weights, *small],
        flops=FLOPS_HINT,
    )
    grad_pieces = gather_pieces(lambda offset: grad_source, attended)
    all_grads = jnp.concatenate(grad_pieces, axis=0)
    middle = flat_tokens + direct_sums(near_sums(output_parts))
    inv_second = lax.rsqrt(jnp.mean(middle * middle, axis=1, keepdims=True) + EPSILON)
    unit_second = middle * inv_second
    normed_own = (unit_second * full_ffn_gain).astype(bfloat)
    normed_pieces = gather_pieces(lambda offset: normed_own)
    normed_second, gate_up_grad, hidden, *feed_parts = whole_call(
        feed_kernel,
        [
            ((total_rows, model_width), bfloat),
            ((total_rows, 2 * hidden_width), bfloat),
            ((total_rows, hidden_width), bfloat),
        ]
        + partial_shapes(total_rows, model_width, team) * 2,
        [*normed_pieces, all_grads, ffn_weights],
        flops=FLOPS_HINT,
    )

    def joined_products(pairs):
        return jnp.concatenate(
            [dot_left(left, right).astype(jnp.bfloat16) for left, right in pairs], axis=1
        )

    def shard_sum(rows):
        return lax.psum_scatter(rows, "shard", scatter_dimension=0, tiled=True)

    second_sums = near_sums(feed_parts[:3])
    down_sums = near_sums([after(part, *second_sums) for part in feed_parts[3:]])
    ffn_terms = joined_products(
        [(normed_second, after(gate_up_grad, *second_sums)), (all_grads, hidden)]
    )
    ffn_rows = shard_sum(ffn_terms)
    normed_grad_second = after(direct_sums(second_sums), ffn_terms)
    ffn_gain_part = jnp.sum(normed_grad_second * unit_second, axis=0)
    unit_grad_second = normed_grad_second * full_ffn_gain
    middle_grad = own_grads.astype(jnp.float32) + inv_second * (
        unit_grad_second
        - unit_second * jnp.mean(unit_grad_second * unit_second, axis=1, keepdims=True)
    )
    grad_own = middle_grad.astype(bfloat)
    down_sums = [after(part, grad_own) for part in down_sums]
    down_sent = [part.astype(bfloat) for part in down_sums]
    middle_pieces = gather_pieces(lambda offset: grad_own, *down_sent)
    middle_grad_b, projected_grad, norm_gain_parts = whole_call(
        attend_back_kernel,
        [
            ((total_rows, model_width), bfloat),
            ((total_rows, qkv_width), bfloat),
            ((8, HEAD_SIZE), jnp.float32),
        ],
        [
            *middle_pieces[:-1],
            middle_pieces[-1],
            projected,
            attended,
            *tables,
            attn_weights,
            *small,
        ],
        [pltpu.VMEM((total_rows, query_width), bfloat)],
        flops=FLOPS_HINT,
    )
    block_sum = middle + direct_sums(down_sums, down_sent)
    block_out = block_sum.astype(bfloat).reshape(sequence_batch, count_of_rows, model_width)

    def rows_for(rows):
        return lambda offset: lax.dynamic_slice_in_dim(
            rows, (ctx_place ^ (offset % ctx_size)) * own_rows, own_rows
        )

    attn_terms = joined_products([(first_normalized, projected_grad), (middle_grad_b, attended)])
    attn_rows = shard_sum(attn_terms)
    ffn_pieces = gather_pieces(rows_for(after(ffn_rows, attn_terms)))
    first_partial = dot_right(after(projected_grad, attn_terms), full_qkv)
    attn_gain_part = jnp.sum(first_partial * unit_first_all, axis=0)
    first_parts = scatter_parts(after(first_partial, *ffn_pieces[1 : team // 2]))
    normed_grad_first = direct_sums(near_sums(first_parts))
    unit_grad_first = normed_grad_first * full_gain
    tokens_grad = middle_grad + inv_first * (
        unit_grad_first
        - unit_first * jnp.mean(unit_grad_first * unit_first, axis=1, keepdims=True)
    )
    tokens_grad = tokens_grad.reshape(sequence_batch, count_of_rows, model_width)
    gain_totals = everyone_sum(
        jnp.concatenate(
            [
                attn_gain_part.reshape(-1, HEAD_SIZE),
                ffn_gain_part.reshape(-1, HEAD_SIZE),
                norm_gain_parts,
            ],
            axis=0,
        )
    )
    gain_rows = model_width // HEAD_SIZE
    attn_gain_grad = lax.dynamic_slice_in_dim(
        gain_totals[:gain_rows].reshape(model_width), own_start, own_rows
    )
    ffn_gain_grad = lax.dynamic_slice_in_dim(
        gain_totals[gain_rows : 2 * gain_rows].reshape(model_width), own_start, own_rows
    )

    ffn_outs = spread_columns(ffn_pieces, member, [hidden_width] * 3)
    gate_weight_grad, up_weight_grad, down_weight_grad = ffn_outs
    attn_rows = after(attn_rows, *ffn_pieces, gain_totals)
    query_weight_grad, key_weight_grad, value_weight_grad, output_weight_grad = spread_columns(
        gather_pieces(rows_for(attn_rows)),
        member,
        [query_width, kv_width, kv_width, query_width],
    )
    return (
        block_out,
        tokens_grad,
        query_weight_grad,
        key_weight_grad,
        value_weight_grad,
        output_weight_grad,
        gate_weight_grad,
        up_weight_grad,
        down_weight_grad,
        attn_gain_grad,
        ffn_gain_grad,
        gain_totals[2 * gain_rows],
        gain_totals[2 * gain_rows + 1],
    )


def solution(mesh):
    in_specs = (
        P(("rep", "shard"), "ctx", None),
        P(("rep", "shard"), "ctx", None),
        P(("rep", "shard"), "ctx"),
        P(),
        P(("shard", "ctx")),
        P(),
        P(),
        P(("shard", "ctx"), None),
        P(("shard", "ctx"), None),
        P(("shard", "ctx"), None),
        P(("shard", "ctx"), None),
        P(("shard", "ctx")),
        P(("shard", "ctx"), None),
        P(("shard", "ctx"), None),
        P(("shard", "ctx"), None),
    )
    out_specs = (
        P(("rep", "shard"), "ctx", None),
        P(("rep", "shard"), "ctx", None),
        P(("shard", "ctx"), None),
        P(("shard", "ctx"), None),
        P(("shard", "ctx"), None),
        P(("shard", "ctx"), None),
        P(("shard", "ctx"), None),
        P(("shard", "ctx"), None),
        P(("shard", "ctx"), None),
        P(("shard", "ctx")),
        P(("shard", "ctx")),
        P(),
        P(),
    )

    return jax.shard_map(
        per_device, mesh=mesh, in_specs=in_specs, out_specs=out_specs, check_vma=False
    )
```

```python
import functools
import math

import jax
import jax.numpy as jnp
from jax import lax
from jax.experimental import pallas as pl
from jax.experimental.pallas import tpu as pltpu
from jax.sharding import PartitionSpec as P

QUERY_HEADS = 16
KEY_VALUE_HEADS = 8
HEAD_SIZE = 128


EPSILON = 1e-06
ROPE_THETA = 1000000.0
NEGATIVE = -1e30
TEAM = ("rep", "ctx")
OWNERS = ("shard", "ctx")
FLOPS_HINT = 8_000_000_000


def plain_product(left_side, right_side):
    return jnp.dot(left_side, right_side, preferred_element_type=jnp.float32)


def dot_right(left_side, right_side):
    return lax.dot_general(
        left_side, right_side, (((1,), (1,)), ((), ())), preferred_element_type=jnp.float32
    )


def dot_left(left_side, right_side):
    return lax.dot_general(
        left_side, right_side, (((0,), (0,)), ((), ())), preferred_element_type=jnp.float32
    )


def axis_bits(axis_name):
    size = lax.axis_size(axis_name)
    assert size & (size - 1) == 0
    return [1 << place for place in range(size.bit_length() - 1)]


def swap(value, axes, offset):
    pairs = [(index, index ^ offset) for index in range(lax.axis_size(axes))]
    return lax.ppermute(value, axes, pairs)


def after(value, *others):
    return lax.optimization_barrier((value,) + others)[0]


def gather_plain(value, axes, offsets):
    blocks = value[None]
    for offset in offsets:
        blocks = jnp.concatenate([blocks, swap(blocks, axes, offset)], axis=0)
    return blocks


def team_layout():
    near = lax.axis_size("ctx")
    members = lax.axis_size(TEAM)
    direct = [offset for offset in range(members) if not offset & near]
    return near, direct, direct + [offset | near for offset in direct]


def gather_pieces(piece_for, *others):
    near, direct, _ = team_layout()
    pieces = [piece_for(0)]
    for offset in direct[:0:-1]:
        pieces.insert(1, swap(piece_for(offset), TEAM, offset))
    if others:
        pieces = [after(piece, *others) for piece in pieces]
    return pieces + [swap(piece, TEAM, near) for piece in pieces]


def near_sums(parts):
    keep, send_last, send_rest = parts
    near = team_layout()[0]
    last = swap(send_last, TEAM, near)
    rest = swap(send_rest, TEAM, near)
    split = send_rest.shape[0]
    return (
        keep[:split] + rest.astype(jnp.float32),
        keep[split:] + last.astype(jnp.float32),
    )


def direct_sums(sums, sent=None):
    rest, last = sent or [part.astype(jnp.bfloat16) for part in sums]
    _, direct, _ = team_layout()
    rows = last.shape[0]
    bands = [rest[place * rows : (place + 1) * rows] for place in range(len(direct) - 1)] + [last]
    total = sums[0][:rows]
    moved = [
        swap(part, TEAM, offset) for offset, part in list(zip(direct, bands))[:0:-1]
    ]
    for part in moved:
        total = total + part.astype(jnp.float32)
    return total


def scatter_parts(value):
    rows = value.shape[0] // lax.axis_size(TEAM)
    half = value.shape[0] // 2
    sent = value[half:].astype(jnp.bfloat16)
    return value[:half], sent[half - rows :], sent[: half - rows]


def everyone_sum(value):
    for axis_name in ("shard", "rep", "ctx"):
        size = lax.axis_size(axis_name)
        if size <= 4:
            moved = [swap(value, axis_name, offset) for offset in range(1, size)]
            value = sum(moved, value)
        else:
            for bit in axis_bits(axis_name):
                value = value + swap(value, axis_name, bit)
    return value


def turned(values, cosine, sine):
    return values * cosine + pltpu.roll(values, HEAD_SIZE // 2, 1) * sine


def unit_rows(values):
    inverse = lax.rsqrt(jnp.mean(values * values, axis=-1, keepdims=True) + EPSILON)
    return (values * inverse, inverse)


def heads_of(projected_ref, cosine, sine, query_gain, key_gain, query_count):
    key_start = query_count * HEAD_SIZE
    queries = []
    for head in range(query_count):
        unit, inverse = unit_rows(projected_ref[:, head * HEAD_SIZE : (head + 1) * HEAD_SIZE])
        queries.append(
            (turned(unit * query_gain, cosine, sine).astype(jnp.bfloat16), unit, inverse)
        )
    key_unit, key_inverse = unit_rows(projected_ref[:, key_start : key_start + HEAD_SIZE])
    key_rot = turned(key_unit * key_gain, cosine, sine).astype(jnp.bfloat16)
    value_rows = projected_ref[:, key_start + HEAD_SIZE : key_start + 2 * HEAD_SIZE].astype(
        jnp.bfloat16
    )
    return queries, (key_rot, key_unit, key_inverse), value_rows


def probabilities(query_rot, key_rot, visible):
    scores = dot_right(query_rot, key_rot) * (1.0 / math.sqrt(HEAD_SIZE))
    scores = jnp.where(visible, scores, NEGATIVE)
    weights = jnp.exp(scores - jnp.max(scores, axis=-1, keepdims=True))
    return weights * (1.0 / jnp.sum(weights, axis=-1, keepdims=True))


def put_partial(value, first, keep_ref, last_ref, rest_ref):
    kept_rows, rest_rows = keep_ref.shape[0], rest_ref.shape[0]
    count = value.shape[0]
    if first < kept_rows:
        keep_ref[first : first + count, :] = value
        return
    start = first - kept_rows
    sent = value.astype(jnp.bfloat16)
    inside = max(0, min(count, rest_rows - start))
    if inside:
        rest_ref[start : start + inside, :] = sent[:inside]
    if inside < count:
        last_start = max(0, start - rest_rows)
        last_ref[last_start : last_start + count - inside, :] = sent[inside:]


def attend_kernel(
    normed_ref,
    cosine_ref,
    sine_ref,
    weights_ref,
    row_ref,
    column_ref,
    query_gain_ref,
    key_gain_ref,
    projected_ref,
    out_ref,
    keep_ref,
    last_ref,
    rest_ref,
):
    query_count = out_ref.shape[1] // HEAD_SIZE
    qkv_width = projected_ref.shape[1]
    length = row_ref.shape[0]
    visible = column_ref[...] <= row_ref[...]
    projected_ref[...] = plain_product(normed_ref[...], weights_ref[:, :qkv_width])
    for first in range(0, normed_ref.shape[0], length):
        rows = slice(first, first + length)
        queries, (key_rot, _, _), value_rows = heads_of(
            projected_ref.at[rows, :],
            cosine_ref[rows, :],
            sine_ref[rows, :],
            query_gain_ref[...],
            key_gain_ref[...],
            query_count,
        )
        for head in range(query_count):
            probs = probabilities(queries[head][0], key_rot, visible).astype(jnp.bfloat16)
            out_ref[rows, head * HEAD_SIZE : (head + 1) * HEAD_SIZE] = plain_product(
                probs, value_rows
            ).astype(jnp.bfloat16)
        put_partial(
            dot_right(out_ref[rows, :], weights_ref[:, qkv_width:]),
            first,
            keep_ref,
            last_ref,
            rest_ref,
        )


def feed_kernel(*refs):
    pieces = refs[:-11]
    (
        grads_ref,
        weights_ref,
        normed_ref,
        gate_up_grad_ref,
        hidden_ref,
        keep_ref,
        last_ref,
        rest_ref,
        down_keep_ref,
        down_last_ref,
        down_rest_ref,
    ) = refs[-11:]
    hidden_width = hidden_ref.shape[1]
    height = pieces[0].shape[0]
    for place, piece in enumerate(pieces):
        normed_ref[place * height : (place + 1) * height, :] = piece[...]
    count = 2 * height
    for first in range(0, normed_ref.shape[0], count):
        rows = slice(first, first + count)
        gate_up = plain_product(normed_ref[rows, :], weights_ref[:, : 2 * hidden_width])
        gate_value = gate_up[:, :hidden_width]
        up_value = gate_up[:, hidden_width:]
        hidden_grad = plain_product(grads_ref[rows, :], weights_ref[:, 2 * hidden_width :])
        sigmoid_gate = jax.nn.sigmoid(gate_value)
        activated = gate_value * sigmoid_gate
        hidden_ref[rows, :] = (activated * up_value).astype(jnp.bfloat16)
        gate_up_grad_ref[rows, :hidden_width] = (
            hidden_grad * up_value * sigmoid_gate * (1.0 + gate_value * (1.0 - sigmoid_gate))
        ).astype(jnp.bfloat16)
        gate_up_grad_ref[rows, hidden_width:] = (hidden_grad * activated).astype(jnp.bfloat16)
        put_partial(
            dot_right(gate_up_grad_ref[rows, :], weights_ref[:, : 2 * hidden_width]),
            first,
            keep_ref,
            last_ref,
            rest_ref,
        )
        put_partial(
            dot_right(hidden_ref[rows, :], weights_ref[:, 2 * hidden_width :]),
            first,
            down_keep_ref,
            down_last_ref,
            down_rest_ref,
        )


def norm_back(gradient, unit, inverse, gain):
    gain_part = jnp.sum(gradient * unit, axis=0, keepdims=True)
    scaled = gradient * gain
    return (
        gain_part,
        inverse * (scaled - unit * jnp.mean(scaled * unit, axis=-1, keepdims=True)),
    )


def attend_back_kernel(*refs):
    pieces = refs[:-13]
    (
        projected_ref,
        attended_ref,
        cosine_ref,
        sine_ref,
        weights_ref,
        row_ref,
        column_ref,
        query_gain_ref,
        key_gain_ref,
        middle_grad_ref,
        out_ref,
        gain_ref,
        grads_ref,
    ) = refs[-13:]
    height = pieces[0].shape[0]
    qkv_width = projected_ref.shape[1]
    length = row_ref.shape[0]
    query_count = attended_ref.shape[1] // HEAD_SIZE
    key_start = query_count * HEAD_SIZE
    visible = column_ref[...] <= row_ref[...]
    scale = 1.0 / math.sqrt(HEAD_SIZE)
    for place, piece in enumerate(pieces):
        middle_grad_ref[place * height : (place + 1) * height, :] = piece[...]
    grads_ref[...] = plain_product(middle_grad_ref[...], weights_ref[:, qkv_width:]).astype(
        jnp.bfloat16
    )
    query_gain_part = jnp.zeros((1, HEAD_SIZE), jnp.float32)
    key_gain_part = jnp.zeros((1, HEAD_SIZE), jnp.float32)
    for first in range(0, projected_ref.shape[0], length):
        rows = slice(first, first + length)
        cosine = cosine_ref[rows, :]
        sine = sine_ref[rows, :]
        queries, (key_rot, key_unit, key_inverse), value_rows = heads_of(
            projected_ref.at[rows, :],
            cosine,
            sine,
            query_gain_ref[...],
            key_gain_ref[...],
            query_count,
        )
        key_grad = jnp.zeros(key_unit.shape, jnp.float32)
        value_grad = jnp.zeros(key_unit.shape, jnp.float32)
        for head in range(query_count):
            columns = slice(head * HEAD_SIZE, (head + 1) * HEAD_SIZE)
            query_rot, query_unit, query_inverse = queries[head]
            grads = grads_ref[rows, columns]
            row_delta = jnp.sum(
                grads.astype(jnp.float32) * attended_ref[rows, columns].astype(jnp.float32),
                axis=-1,
                keepdims=True,
            )
            prob_float = probabilities(query_rot, key_rot, visible)
            value_grad = value_grad + dot_left(prob_float.astype(jnp.bfloat16), grads)
            score_grad = (prob_float * (dot_right(grads, value_rows) - row_delta)).astype(
                jnp.bfloat16
            )
            query_grad = plain_product(score_grad, key_rot) * scale
            key_grad = key_grad + dot_left(score_grad, query_rot)
            part, query_pre = norm_back(
                turned(query_grad, cosine, -sine), query_unit, query_inverse, query_gain_ref[...]
            )
            query_gain_part = query_gain_part + part
            out_ref[rows, columns] = query_pre.astype(jnp.bfloat16)
        part, key_pre = norm_back(
            turned(key_grad * scale, cosine, -sine), key_unit, key_inverse, key_gain_ref[...]
        )
        key_gain_part = key_gain_part + part
        out_ref[rows, key_start : key_start + HEAD_SIZE] = key_pre.astype(jnp.bfloat16)
        out_ref[rows, key_start + HEAD_SIZE : key_start + 2 * HEAD_SIZE] = value_grad.astype(
            jnp.bfloat16
        )
    gain_ref[...] = jnp.zeros_like(gain_ref)
    gain_ref[0:1, :] = query_gain_part
    gain_ref[1:2, :] = key_gain_part


def whole_call(kernel, out_shapes, operands, scratch=(), flops=0):
    moved = sum(math.prod(shape) * jnp.dtype(kind).itemsize for shape, kind in out_shapes)
    moved += sum(array.size * array.dtype.itemsize for array in operands)
    return pl.pallas_call(
        kernel,
        in_specs=[pl.BlockSpec(memory_space=pltpu.VMEM)] * len(operands),
        out_specs=[pl.BlockSpec(memory_space=pltpu.VMEM)] * len(out_shapes),
        out_shape=[jax.ShapeDtypeStruct(shape, kind) for shape, kind in out_shapes],
        scratch_shapes=list(scratch),
        cost_estimate=pl.CostEstimate(flops=flops, transcendentals=0, bytes_accessed=moved),
    )(*operands)


def partial_shapes(rows, width, members):
    own = rows // members
    return [
        ((rows // 2, width), jnp.float32),
        ((own, width), jnp.bfloat16),
        ((rows // 2 - own, width), jnp.bfloat16),
    ]


def spread_kernel(member_ref, *refs, widths, offsets):
    blocks, out_refs = refs[: len(offsets)], refs[len(offsets) :]
    for block, offset in zip(blocks, offsets):
        place = member_ref[0] ^ offset
        start = 0
        for out_ref, width in zip(out_refs, widths):
            first = pl.multiple_of(place * width, width)
            out_ref[:, pl.ds(first, width)] = block[:, start : start + width].astype(jnp.float32)
            start += width


def spread_columns(blocks, member, widths):
    offsets = team_layout()[2]
    rows = blocks[0].shape[0]
    return pl.pallas_call(
        functools.partial(spread_kernel, widths=widths, offsets=offsets),
        in_specs=[pl.BlockSpec(memory_space=pltpu.SMEM)]
        + [pl.BlockSpec(memory_space=pltpu.VMEM)] * len(blocks),
        out_specs=[pl.BlockSpec(memory_space=pltpu.VMEM)] * len(widths),
        out_shape=[
            jax.ShapeDtypeStruct((rows, size * len(blocks)), jnp.float32) for size in widths
        ],
    )(member.reshape(1), *blocks)


def per_device(
    tokens,
    out_grad,
    positions,
    stretch_order,
    attn_gain,
    query_gain,
    key_norm_gain,
    query_weight,
    key_projection_matrix,
    value_projection_matrix,
    output_weight,
    ffn_gain,
    gate_weight,
    up_weight,
    down_weight,
):
    sequence_batch, count_of_rows, model_width = tokens.shape
    local_rows = sequence_batch * count_of_rows
    team = lax.axis_size(TEAM)
    ctx_size = lax.axis_size("ctx")
    ctx_place = lax.axis_index("ctx")
    member = lax.axis_index(TEAM)
    axis_offsets = [1 << bit for bit in range(team.bit_length() - 1)]
    query_width = QUERY_HEADS // team * HEAD_SIZE
    kv_width = KEY_VALUE_HEADS // team * HEAD_SIZE
    hidden_width = gate_weight.shape[1] // team
    own_rows = model_width // lax.axis_size(OWNERS)
    own_start = lax.axis_index(OWNERS) * own_rows

    def ctx_columns(matrices, place):
        start_member = lax.axis_index("rep") * ctx_size + place
        pieces = []
        for matrix in matrices:
            width = matrix.shape[1] // team
            pieces.append(
                lax.dynamic_slice_in_dim(matrix, start_member * width, width, axis=1)
            )
        return jnp.concatenate(pieces, axis=1)

    def ctx_exchange(pick, axis, *others):
        received = [pick(ctx_place)]
        for offset in range(1, ctx_size):
            received.append(swap(after(pick(ctx_place ^ offset), *others), "ctx", offset))
        if ctx_size == 1:
            return received[0]
        if ctx_size == 2:
            return jnp.where(
                ctx_place == 0,
                jnp.concatenate(received, axis=axis),
                jnp.concatenate(received[::-1], axis=axis),
            )
        stacked = jnp.stack(received)
        return jnp.concatenate(
            [
                lax.dynamic_index_in_dim(stacked, ctx_place ^ place, 0, keepdims=False)
                for place in range(ctx_size)
            ],
            axis=axis,
        )

    def team_rows(matrices, *others):
        return ctx_exchange(lambda place: ctx_columns(matrices, place), 0, *others)

    def all_rows(rows):
        return lax.all_gather(rows, "shard", axis=0, tiled=True)

    attn_part = team_rows(
        [query_weight, key_projection_matrix, value_projection_matrix, output_weight]
    )
    ffn_part = team_rows([gate_weight, up_weight, down_weight], attn_part)
    attn_weights = all_rows(attn_part)
    ffn_weights = all_rows(ffn_part)
    qkv_width = query_width + 2 * kv_width
    full_qkv = attn_weights[:, :qkv_width]
    owners = lax.axis_size(OWNERS)
    gain_blocks = gather_plain(
        jnp.stack([attn_gain, ffn_gain]),
        OWNERS, [1 << bit for bit in range(owners.bit_length() - 1)]
    )
    owner_places = jnp.arange(owners, dtype=jnp.int32)
    from_block = (owner_places[:, None] ^ lax.axis_index(OWNERS)) == owner_places[None, :]
    gains = jnp.einsum(
        "jk,kgf->gjf",
        from_block.astype(jnp.bfloat16),
        gain_blocks,
        preferred_element_type=jnp.float32,
    ).reshape(2, 1, model_width)
    full_gain = gains[0]
    full_ffn_gain = gains[1]

    own_tokens = tokens.reshape(local_rows, model_width)
    own_grads = out_grad.reshape(local_rows, model_width)
    token_source = after(own_tokens, attn_part)
    token_pieces = gather_pieces(lambda offset: token_source)
    all_tokens = jnp.concatenate(token_pieces, axis=0)
    grad_source = after(own_grads, *token_pieces)
    total_rows = all_tokens.shape[0]
    assert sequence_batch == 1

    half_size = HEAD_SIZE // 2
    freq_steps = jnp.arange(HEAD_SIZE, dtype=jnp.int32)
    inverse = jnp.exp(
        (freq_steps % half_size).astype(jnp.float32) * (-2.0 * math.log(ROPE_THETA) / HEAD_SIZE)
    )
    all_positions = gather_plain(
        after(positions, token_pieces[1]),
        TEAM,
        [bit for bit in axis_offsets if bit != ctx_size] + [ctx_size],
    ).reshape(total_rows)
    angles = all_positions.astype(jnp.float32)[:, None] * inverse[None, :]
    tables = (
        jnp.cos(angles),
        jnp.sin(angles) * jnp.where(freq_steps < half_size, -1.0, 1.0)[None, :],
    )

    stretches_here = stretch_order.shape[0] // ctx_size
    block_rows = count_of_rows // stretches_here
    local = jnp.arange(count_of_rows, dtype=jnp.int32)
    match = (local // block_rows)[:, None] == jnp.arange(stretches_here, dtype=jnp.int32)[None]

    def stored_index(place):
        blocks = lax.dynamic_slice_in_dim(stretch_order, place * stretches_here, stretches_here)
        return (
            jnp.sum(jnp.where(match, blocks[None, :], 0), axis=1) * block_rows + local % block_rows
        )

    seq_index = jnp.concatenate([stored_index(ctx_place ^ offset) for offset in range(ctx_size)])
    small = (
        seq_index[:, None],
        seq_index[None, :],
        query_gain.astype(jnp.float32)[None, :],
        key_norm_gain.astype(jnp.float32)[None, :],
    )

    float_tokens = all_tokens.astype(jnp.float32)
    inv_first_all = lax.rsqrt(
        jnp.mean(float_tokens * float_tokens, axis=1, keepdims=True) + EPSILON
    )
    unit_first_all = float_tokens * inv_first_all
    first_normalized = (unit_first_all * full_gain).astype(jnp.bfloat16)
    flat_tokens = own_tokens.astype(jnp.float32)
    inv_first = inv_first_all[:local_rows]
    unit_first = flat_tokens * inv_first
    bfloat = jnp.bfloat16
    projected, attended, *output_parts = whole_call(
        attend_kernel,
        [((total_rows, qkv_width), jnp.float32), ((total_rows, query_width), bfloat)]
        + partial_shapes(total_rows, model_width, team),
        [after(first_normalized, ffn_part), *tables, attn_weights, *small],
        flops=FLOPS_HINT,
    )
    grad_pieces = gather_pieces(lambda offset: grad_source, attended)
    all_grads = jnp.concatenate(grad_pieces, axis=0)
    middle = flat_tokens + direct_sums(near_sums(output_parts))
    inv_second = lax.rsqrt(jnp.mean(middle * middle, axis=1, keepdims=True) + EPSILON)
    unit_second = middle * inv_second
    normed_own = (unit_second * full_ffn_gain).astype(bfloat)
    normed_pieces = gather_pieces(lambda offset: normed_own)
    normed_second, gate_up_grad, hidden, *feed_parts = whole_call(
        feed_kernel,
        [
            ((total_rows, model_width), bfloat),
            ((total_rows, 2 * hidden_width), bfloat),
            ((total_rows, hidden_width), bfloat),
        ]
        + partial_shapes(total_rows, model_width, team) * 2,
        [*normed_pieces, all_grads, ffn_weights],
        flops=FLOPS_HINT,
    )

    def joined_products(pairs):
        return jnp.concatenate(
            [dot_left(left, right).astype(jnp.bfloat16) for left, right in pairs], axis=1
        )

    def shard_sum(rows):
        return lax.psum_scatter(rows, "shard", scatter_dimension=0, tiled=True)

    second_sums = near_sums(feed_parts[:3])
    down_sums = near_sums([after(part, *second_sums) for part in feed_parts[3:]])
    down_terms = dot_left(all_grads, hidden).astype(bfloat)
    gate_up_terms = dot_left(normed_second, after(gate_up_grad, *second_sums)).astype(bfloat)
    ffn_terms = jnp.concatenate([gate_up_terms, down_terms], axis=1)
    ffn_rows = shard_sum(ffn_terms)
    normed_grad_second = after(direct_sums(second_sums), ffn_terms)
    ffn_gain_part = jnp.sum(normed_grad_second * unit_second, axis=0)
    unit_grad_second = normed_grad_second * full_ffn_gain
    middle_grad = own_grads.astype(jnp.float32) + inv_second * (
        unit_grad_second
        - unit_second * jnp.mean(unit_grad_second * unit_second, axis=1, keepdims=True)
    )
    grad_own = middle_grad.astype(bfloat)
    down_sums = [after(part, grad_own) for part in down_sums]
    down_sent = [part.astype(bfloat) for part in down_sums]
    middle_pieces = gather_pieces(lambda offset: grad_own, *down_sent)
    middle_grad_b, projected_grad, norm_gain_parts = whole_call(
        attend_back_kernel,
        [
            ((total_rows, model_width), bfloat),
            ((total_rows, qkv_width), bfloat),
            ((8, HEAD_SIZE), jnp.float32),
        ],
        [
            *middle_pieces[:-1],
            middle_pieces[-1],
            projected,
            attended,
            *tables,
            attn_weights,
            *small,
        ],
        [pltpu.VMEM((total_rows, query_width), bfloat)],
        flops=FLOPS_HINT,
    )
    block_sum = middle + direct_sums(down_sums, down_sent)
    block_out = block_sum.astype(bfloat).reshape(sequence_batch, count_of_rows, model_width)

    def rows_for(rows):
        return lambda offset: lax.dynamic_slice_in_dim(
            rows, (ctx_place ^ (offset % ctx_size)) * own_rows, own_rows
        )

    attn_terms = joined_products([(first_normalized, projected_grad), (middle_grad_b, attended)])
    attn_rows = shard_sum(attn_terms)
    ffn_sent = {
        offset: rows_for(after(ffn_rows, attn_terms))(offset) for offset in team_layout()[1]
    }
    ffn_pieces = gather_pieces(lambda offset: ffn_sent[offset])
    first_partial = dot_right(after(projected_grad, attn_terms, *ffn_sent.values()), full_qkv)
    attn_gain_part = jnp.sum(first_partial * unit_first_all, axis=0)
    gain_totals = everyone_sum(
        jnp.concatenate(
            [
                attn_gain_part.reshape(-1, HEAD_SIZE),
                ffn_gain_part.reshape(-1, HEAD_SIZE),
                norm_gain_parts,
            ],
            axis=0,
        )
    )
    first_parts = scatter_parts(after(first_partial, *ffn_pieces[1 : team // 2]))
    normed_grad_first = direct_sums(near_sums(first_parts))
    unit_grad_first = normed_grad_first * full_gain
    tokens_grad = middle_grad + inv_first * (
        unit_grad_first
        - unit_first * jnp.mean(unit_grad_first * unit_first, axis=1, keepdims=True)
    )
    tokens_grad = tokens_grad.reshape(sequence_batch, count_of_rows, model_width)
    gain_rows = model_width // HEAD_SIZE
    attn_gain_grad = lax.dynamic_slice_in_dim(
        gain_totals[:gain_rows].reshape(model_width), own_start, own_rows
    )
    ffn_gain_grad = lax.dynamic_slice_in_dim(
        gain_totals[gain_rows : 2 * gain_rows].reshape(model_width), own_start, own_rows
    )

    ffn_outs = spread_columns(ffn_pieces, member, [hidden_width] * 3)
    gate_weight_grad, up_weight_grad, down_weight_grad = ffn_outs
    attn_rows = after(attn_rows, *ffn_pieces)
    query_weight_grad, key_weight_grad, value_weight_grad, output_weight_grad = spread_columns(
        gather_pieces(rows_for(attn_rows)),
        member,
        [query_width, kv_width, kv_width, query_width],
    )
    return (
        block_out,
        tokens_grad,
        query_weight_grad,
        key_weight_grad,
        value_weight_grad,
        output_weight_grad,
        gate_weight_grad,
        up_weight_grad,
        down_weight_grad,
        attn_gain_grad,
        ffn_gain_grad,
        gain_totals[2 * gain_rows],
        gain_totals[2 * gain_rows + 1],
    )


def solution(mesh):
    in_specs = (
        P(("rep", "shard"), "ctx", None),
        P(("rep", "shard"), "ctx", None),
        P(("rep", "shard"), "ctx"),
        P(),
        P(("shard", "ctx")),
        P(),
        P(),
        P(("shard", "ctx"), None),
        P(("shard", "ctx"), None),
        P(("shard", "ctx"), None),
        P(("shard", "ctx"), None),
        P(("shard", "ctx")),
        P(("shard", "ctx"), None),
        P(("shard", "ctx"), None),
        P(("shard", "ctx"), None),
    )
    out_specs = (
        P(("rep", "shard"), "ctx", None),
        P(("rep", "shard"), "ctx", None),
        P(("shard", "ctx"), None),
        P(("shard", "ctx"), None),
        P(("shard", "ctx"), None),
        P(("shard", "ctx"), None),
        P(("shard", "ctx"), None),
        P(("shard", "ctx"), None),
        P(("shard", "ctx"), None),
        P(("shard", "ctx")),
        P(("shard", "ctx")),
        P(),
        P(),
    )

    return jax.shard_map(
        per_device, mesh=mesh, in_specs=in_specs, out_specs=out_specs, check_vma=False
    )
```
